512 devices in a mesh: seq: 128 (over y, z, core), dp: 4 (over x).
Axes of the slice: x: 4, y: 8, z: 8, core: 2. Of those that a mesh axis runs over, the one named last changes fastest.
Arguments:
- layer_inputs: bfloat16 [4, 32768, 4096], P('dp', 'seq')
- doc_start: int32 [4, 32768], P('dp', 'seq'), may hold values from 0 to 32767, as said below
- w_qkv: bfloat16 [4096, 512], P(('seq', 'dp'))
- d_context: bfloat16 [4, 32768, 256], P('dp', 'seq'), may hold values from -6 to 6
Outputs:
- d_x: bfloat16 [4, 32768, 4096], P('dp', 'seq')
- g_qkv: float32 [4096, 512], P(('seq', 'dp'))
The draws below stay inside these ranges and needn't reach their ends.
Inputs may be any that keep to these rules, and one draw needn't show every extreme that they name: doc_start[g, i] is at most i, never falls along positions, doc_start[g, 0] = 0, and doc_start[g, doc_start[g, i]] = doc_start[g, i].
All inputs are finite; a program needn't handle non-finite values.
Results may differ from the reference program's by a relative error of at most 0.017.
Values may be sent and summed in bfloat16 or wider, within the bound.
No kernel may reach another device: no remote copies, remote signals or barrier semaphores. Data moves between devices by JAX's collectives and lax.ppermute only.
A program may use at most 64 MiB of HBM per device.

```python
import jax
import jax.numpy as jnp
from jax import lax

D = 4096
HD = 128
QH = 2
TOK_DEV = 256
WIN = 256
GROUPS = 4
TOKENS = 32768
N_SEQ = 128


def draw_layer_inputs(key, part):
    full_shape = (GROUPS, TOKENS, D)
    values = jax.random.normal(jax.random.fold_in(key, 21), full_shape, jnp.float32)
    return jnp.clip(values, -6.0, 6.0).astype(jnp.bfloat16)


def draw_w_qkv(key, part):
    q_width = QH * HD
    table_fresh = jax.random.normal(jax.random.fold_in(key, 31), (D, q_width + 2 * HD), jnp.float32) * D ** (-0.5)
    return table_fresh.astype(jnp.bfloat16)


def draw_doc_start(key, part):
    start_marks = jax.random.randint(jax.random.fold_in(key, 41), (GROUPS, TOKENS), 0, TOK_DEV)
    position_index = jnp.arange(TOKENS, dtype=jnp.int32)[None, :]
    opening = (start_marks == 0) | (position_index == 0) | (position_index == TOKENS - 1)
    return lax.cummax(jnp.where(opening, position_index, 0), axis=1).astype(jnp.int32)


def block_scale(own_key, dims, pieces, least, top_value):
    def one(dim, blocks):
        steps = jax.random.uniform(jax.random.fold_in(jax.random.fold_in(own_key, 6), dim), (blocks,), jnp.float32, least / len(pieces), top_value / len(pieces))
        return jnp.repeat(jnp.exp(steps), dims[dim] // blocks).reshape((-1,) + (1,) * (len(dims) - dim - 1))

    level = one(*pieces[0])
    for cut in pieces[1:]:
        level = level * one(*cut)
    return level


def normal_values(key, dims, deviation, limit, cuts=(), kind=jnp.bfloat16):
    array = deviation * jax.random.normal(key, dims, jnp.float32)
    if cuts:
        array = array * block_scale(key, dims, cuts, -0.22, 0.18)
    return jnp.clip(array, -limit, limit).astype(kind)


def setup_inputs(seed: int = 0) -> dict:
    splits = jax.random.split(jax.random.key(seed), 5)
    layer_inputs = draw_layer_inputs(jax.random.fold_in(splits[4], 71), 0)
    doc_start = draw_doc_start(jax.random.fold_in(splits[4], 71), 0)
    w_qkv = draw_w_qkv(jax.random.fold_in(splits[4], 71), 0)
    d_context = normal_values(splits[3], (GROUPS, TOKENS, QH * HD), 1.0, 6.0, ((0, 4), (1, 128)))
    return dict(layer_inputs=layer_inputs, doc_start=doc_start, w_qkv=w_qkv, d_context=d_context)


def masked_scores(queries, key_rows, doc_first, query_pos, key_pos):
    inv_root = queries.shape[2] ** -0.5
    scores = jnp.einsum("rhd,kd->hrk", queries.astype(jnp.float32), key_rows.astype(jnp.float32)) * inv_root
    visible = (key_pos[None, :] <= query_pos[:, None]) & (key_pos[None, :] > query_pos[:, None] - WIN) & (key_pos[None, :] >= doc_first[:, None])
    return jnp.where(visible[None, :, :], scores, -jnp.inf)


def backward_terms(queries, key_rows, value_rows, out_grad, attn_probs, prob_low, row_dot):
    inv_root = queries.shape[2] ** -0.5
    prob_grad = jnp.einsum("rhd,kd->hrk", out_grad.astype(jnp.float32), value_rows.astype(jnp.float32))
    score_grad = (attn_probs * (prob_grad - row_dot[:, :, None])).astype(jnp.bfloat16)
    grad_query = jnp.einsum("hrk,kd->rhd", score_grad.astype(jnp.float32), key_rows.astype(jnp.float32)) * inv_root
    grad_keys = jnp.einsum("hrk,rhd->kd", score_grad.astype(jnp.float32), queries.astype(jnp.float32)) * inv_root
    grad_values = jnp.einsum("hrk,rhd->kd", prob_low.astype(jnp.float32), out_grad.astype(jnp.float32))
    return grad_query, grad_keys, grad_values


def local_pass(queries, key_rows, value_rows, out_grad, doc_first, query_pos, key_pos):
    scores = masked_scores(queries, key_rows, doc_first, query_pos, key_pos)
    row_max = jnp.max(scores, axis=2)
    log_total = row_max + jnp.log(jnp.sum(jnp.exp(scores - row_max[:, :, None]), axis=2))
    attn_probs = jnp.exp(scores - log_total[:, :, None])
    prob_low = attn_probs.astype(jnp.bfloat16)
    context = jnp.einsum("hrk,kd->rhd", prob_low.astype(jnp.float32), value_rows.astype(jnp.float32))
    row_dot = jnp.sum(out_grad.astype(jnp.float32) * context, axis=2).T
    return backward_terms(queries, key_rows, value_rows, out_grad, attn_probs, prob_low, row_dot)


def reference(layer_inputs, doc_start, w_qkv, d_context):
    q_width = QH * HD
    positions = jnp.arange(TOKENS, dtype=jnp.int32).reshape(N_SEQ, TOK_DEV)
    key_pos = jnp.concatenate([positions - TOK_DEV, positions], axis=1)
    grad_total = jnp.zeros((D, (QH + 2) * HD), jnp.float32)
    input_grads = []
    for group_index in range(GROUPS):
        x_group = layer_inputs[group_index]
        projected = jnp.dot(x_group, w_qkv, preferred_element_type=jnp.float32).astype(jnp.bfloat16)
        queries = projected[:, :q_width].reshape(N_SEQ, TOK_DEV, QH, HD)
        key_own = projected[:, q_width:q_width + HD].reshape(N_SEQ, TOK_DEV, HD)
        value_own = projected[:, q_width + HD:].reshape(N_SEQ, TOK_DEV, HD)
        zero_rows = jnp.zeros((1, TOK_DEV, HD), jnp.bfloat16)
        key_rows = jnp.concatenate([jnp.concatenate([zero_rows, key_own[:-1]], axis=0), key_own], axis=1)
        value_rows = jnp.concatenate([jnp.concatenate([zero_rows, value_own[:-1]], axis=0), value_own], axis=1)
        out_grad = d_context[group_index].reshape(N_SEQ, TOK_DEV, QH, HD)
        doc_first = doc_start[group_index].reshape(N_SEQ, TOK_DEV)

        def one_block(block_item):
            return local_pass(*block_item)

        grad_query, grad_keys, grad_values = lax.map(one_block, (queries, key_rows, value_rows, out_grad, doc_first, positions, key_pos))
        float_zero = jnp.zeros((1, TOK_DEV, HD), jnp.float32)
        key_total = grad_keys[:, TOK_DEV:] + jnp.concatenate([grad_keys[1:, :TOK_DEV], float_zero], axis=0)
        value_total = grad_values[:, TOK_DEV:] + jnp.concatenate([grad_values[1:, :TOK_DEV], float_zero], axis=0)
        grad_proj = jnp.concatenate([
            grad_query.astype(jnp.bfloat16).reshape(TOKENS, q_width),
            key_total.astype(jnp.bfloat16).reshape(TOKENS, HD),
            value_total.astype(jnp.bfloat16).reshape(TOKENS, HD)], axis=1)
        input_grads.append(lax.dot_general(grad_proj, w_qkv, (((1,), (1,)), ((), ())), preferred_element_type=jnp.float32).astype(jnp.bfloat16))
        grad_total = grad_total + lax.dot_general(x_group, grad_proj, (((0,), (0,)), ((), ())), preferred_element_type=jnp.float32)
    return jnp.stack(input_grads), grad_total
```

```python
import jax
import jax.numpy as jnp
from jax import lax
from jax.sharding import PartitionSpec as P

WIN = 256


def from_behind(block, axis, distance):
    devices = range(lax.axis_size(axis))
    route = [(i - distance, i) for i in devices if i - distance in devices]
    return lax.ppermute(block, axis, route)


def masked_scores(queries, key_rows, doc_first, query_pos, key_pos):
    inv_root = queries.shape[2] ** (-0.5)
    scores = (
        jnp.einsum("rhd,kd->hrk", queries, key_rows, preferred_element_type=jnp.float32) * inv_root
    )
    visible = (
        (key_pos[None, :] <= query_pos[:, None])
        & (key_pos[None, :] > query_pos[:, None] - WIN)
        & (key_pos[None, :] >= doc_first[:, None])
    )
    return jnp.where(visible[None, :, :], scores, -jnp.inf)


def backward_terms(queries, key_rows, value_rows, out_grad, attn_probs, prob_low, row_dot):
    inv_root = queries.shape[2] ** (-0.5)
    prob_grad = jnp.einsum("rhd,kd->hrk", out_grad, value_rows, preferred_element_type=jnp.float32)
    score_grad = (attn_probs * (prob_grad - row_dot[:, :, None])).astype(jnp.bfloat16)
    grad_query = (
        jnp.einsum("hrk,kd->rhd", score_grad, key_rows, preferred_element_type=jnp.float32)
        * inv_root
    )
    grad_keys = (
        jnp.einsum("hrk,rhd->kd", score_grad, queries, preferred_element_type=jnp.float32)
        * inv_root
    )
    grad_values = jnp.einsum("hrk,rhd->kd", prob_low, out_grad, preferred_element_type=jnp.float32)
    return (grad_query, grad_keys, grad_values)


def local_pass(queries, key_rows, value_rows, out_grad, doc_first, query_pos, key_pos):
    scores = masked_scores(queries, key_rows, doc_first, query_pos, key_pos)
    row_max = jnp.max(scores, axis=2)
    log_total = row_max + jnp.log(jnp.sum(jnp.exp(scores - row_max[:, :, None]), axis=2))
    attn_probs = jnp.exp(scores - log_total[:, :, None])
    prob_low = attn_probs.astype(jnp.bfloat16)
    context = jnp.einsum("hrk,kd->rhd", prob_low, value_rows, preferred_element_type=jnp.float32)
    row_dot = jnp.sum(out_grad.astype(jnp.float32) * context, axis=2).T
    grad_query, grad_keys, grad_values = backward_terms(
        queries, key_rows, value_rows, out_grad, attn_probs, prob_low, row_dot
    )
    return (grad_query, grad_keys, grad_values, log_total, row_dot)


AXES = ("seq", "dp")


def spot(y, z, core, x):
    return ((y % 8 * 8 + z % 8) * 2 + core) * 4 + x % 4


def far_groups():
    return [
        [spot(2 * y + a, 2 * z + b, core, 2 * x + d) for y in range(4) for z in range(4) for x in range(2)]
        for a in range(2)
        for b in range(2)
        for core in range(2)
        for d in range(2)
    ]


def near_groups():
    groups = []
    for core in range(2):
        for y in range(4):
            for z in range(4):
                for x in range(2):
                    low = [(k, k) if core == 0 else (k, 2 - k) for k in range(2)]
                    groups.append(
                        [
                            spot(2 * y + a[1], 2 * z + b[1], core, 2 * x + d[1])
                            for a in low
                            for b in low
                            for d in low
                        ]
                    )
    return groups


def exchange(blocks, groups):
    return lax.all_to_all(blocks, AXES, 0, 0, axis_index_groups=groups)


def swap_cores(block):
    count = lax.axis_size("seq")
    return lax.ppermute(block, "seq", [(i, i ^ 1) for i in range(count)])


def gather_weights(w_block):
    rows, width = w_block.shape
    far = exchange(jnp.broadcast_to(w_block, (32, rows, width)), far_groups())
    far = far.reshape(32 * rows, width)
    own = exchange(jnp.broadcast_to(far, (8,) + far.shape), near_groups())
    other = swap_cores(own)
    core = lax.axis_index("seq") & 1
    both = jnp.stack([jnp.where(core == 0, own, other), jnp.where(core == 0, other, own)])
    both = both.reshape(2, 2, 2, 2, 4, 4, 2, rows, width)
    return both.transpose(4, 1, 5, 2, 0, 6, 3, 7, 8).reshape(512 * rows, width)


def scatter_sum(partial):
    rows, width = partial.shape[0] // 512, partial.shape[1]
    core = lax.axis_index("seq") & 1
    split = partial.reshape(4, 2, 4, 2, 2, 2, 2, rows, width)

    def half(which):
        part = lax.dynamic_index_in_dim(split, which, 4, keepdims=False)
        return part.transpose(1, 3, 5, 0, 2, 4, 6, 7).reshape(8, 32 * rows, width)

    received = swap_cores(half(1 - core).astype(jnp.bfloat16))
    total = (half(core) + received.astype(jnp.float32)).astype(jnp.bfloat16)
    total = jnp.sum(exchange(total, near_groups()).astype(jnp.float32), axis=0)
    total = total.astype(jnp.bfloat16).reshape(32, rows, width)
    return jnp.sum(exchange(total, far_groups()).astype(jnp.float32), axis=0)


def body(layer_inputs, doc_start, w_qkv, d_context):
    x_local = layer_inputs[0]
    tok_rows = x_local.shape[0]
    q_width = d_context.shape[2]
    head_dim = (w_qkv.shape[1] - q_width) // 2
    heads = q_width // head_dim
    out_grad = d_context[0].reshape(tok_rows, heads, head_dim)
    doc_first = doc_start[0]
    positions = lax.axis_index("seq") * tok_rows + jnp.arange(tok_rows, dtype=jnp.int32)
    full_weights = gather_weights(w_qkv)
    projected = jnp.dot(x_local, full_weights, preferred_element_type=jnp.float32)
    projected = projected.astype(jnp.bfloat16)
    queries = projected[:, :q_width].reshape(tok_rows, heads, head_dim)
    key_value = projected[:, q_width:]
    prior = from_behind(key_value, "seq", 1)
    key_rows = jnp.concatenate([prior[:, :head_dim], key_value[:, :head_dim]], axis=0)
    value_rows = jnp.concatenate([prior[:, head_dim:], key_value[:, head_dim:]], axis=0)
    key_pos = jnp.concatenate([positions - tok_rows, positions])
    grad_query, grad_keys, grad_values, log_total, row_dot = local_pass(
        queries, key_rows, value_rows, out_grad, doc_first, positions, key_pos
    )
    returned = from_behind(
        jnp.concatenate([grad_keys[:tok_rows], grad_values[:tok_rows]], axis=1).astype(
            jnp.bfloat16
        ),
        "seq",
        -1,
    ).astype(jnp.float32)
    far_keys = returned[:, :head_dim]
    far_values = returned[:, head_dim:]
    key_grad = (grad_keys[tok_rows:] + far_keys).astype(jnp.bfloat16)
    value_grad = (grad_values[tok_rows:] + far_values).astype(jnp.bfloat16)
    grad_proj = jnp.concatenate(
        [grad_query.astype(jnp.bfloat16).reshape(tok_rows, q_width), key_grad, value_grad], axis=1
    )
    input_grad = lax.dot_general(
        grad_proj, full_weights, (((1,), (1,)), ((), ())), preferred_element_type=jnp.float32
    )
    input_grad = input_grad.astype(jnp.bfloat16).reshape(1, tok_rows, x_local.shape[1])
    partial_grad = lax.dot_general(
        x_local, grad_proj, (((0,), (0,)), ((), ())), preferred_element_type=jnp.float32
    )
    return (input_grad, scatter_sum(partial_grad))


def solution(mesh):
    return jax.shard_map(
        body,
        mesh=mesh,
        in_specs=(
            P("dp", "seq", None),
            P("dp", "seq"),
            P(("seq", "dp"), None),
            P("dp", "seq", None),
        ),
        out_specs=(P("dp", "seq", None), P(("seq", "dp"), None)),
        check_vma=False,
    )
```

```python
import jax
import jax.numpy as jnp
from jax import lax
from jax.sharding import PartitionSpec as P

WIN = 256


def from_behind(block, axis, distance):
    devices = range(lax.axis_size(axis))
    route = [(i - distance, i) for i in devices if i - distance in devices]
    return lax.ppermute(block, axis, route)


def masked_scores(queries, key_rows, doc_first, query_pos, key_pos):
    inv_root = queries.shape[2] ** (-0.5)
    scores = (
        jnp.einsum("rhd,kd->hrk", queries, key_rows, preferred_element_type=jnp.float32) * inv_root
    )
    visible = (
        (key_pos[None, :] <= query_pos[:, None])
        & (key_pos[None, :] > query_pos[:, None] - WIN)
        & (key_pos[None, :] >= doc_first[:, None])
    )
    return jnp.where(visible[None, :, :], scores, -jnp.inf)


def backward_terms(queries, key_rows, value_rows, out_grad, attn_probs, prob_low, row_dot):
    inv_root = queries.shape[2] ** (-0.5)
    prob_grad = jnp.einsum("rhd,kd->hrk", out_grad, value_rows, preferred_element_type=jnp.float32)
    score_grad = (attn_probs * (prob_grad - row_dot[:, :, None])).astype(jnp.bfloat16)
    grad_query = (
        jnp.einsum("hrk,kd->rhd", score_grad, key_rows, preferred_element_type=jnp.float32)
        * inv_root
    )
    grad_keys = (
        jnp.einsum("hrk,rhd->kd", score_grad, queries, preferred_element_type=jnp.float32)
        * inv_root
    )
    grad_values = jnp.einsum("hrk,rhd->kd", prob_low, out_grad, preferred_element_type=jnp.float32)
    return (grad_query, grad_keys, grad_values)


def local_pass(queries, key_rows, value_rows, out_grad, doc_first, query_pos, key_pos):
    scores = masked_scores(queries, key_rows, doc_first, query_pos, key_pos)
    row_max = jnp.max(scores, axis=2)
    log_total = row_max + jnp.log(jnp.sum(jnp.exp(scores - row_max[:, :, None]), axis=2))
    attn_probs = jnp.exp(scores - log_total[:, :, None])
    prob_low = attn_probs.astype(jnp.bfloat16)
    context = jnp.einsum("hrk,kd->rhd", prob_low, value_rows, preferred_element_type=jnp.float32)
    row_dot = jnp.sum(out_grad.astype(jnp.float32) * context, axis=2).T
    grad_query, grad_keys, grad_values = backward_terms(
        queries, key_rows, value_rows, out_grad, attn_probs, prob_low, row_dot
    )
    return (grad_query, grad_keys, grad_values, log_total, row_dot)


AXES = ("seq", "dp")


def spot(y, z, core, x):
    return ((y % 8 * 8 + z % 8) * 2 + core) * 4 + x % 4


def far_groups():
    return [
        [spot(2 * y + a, 2 * z + b, core, 2 * x + d) for y in range(4) for z in range(4) for x in range(2)]
        for a in range(2)
        for b in range(2)
        for core in range(2)
        for d in range(2)
    ]


def near_groups():
    groups = []
    for core in range(2):
        for y in range(4):
            for z in range(4):
                for x in range(2):
                    low = [(k, k) if core == 0 else (k, 2 - k) for k in range(2)]
                    groups.append(
                        [
                            spot(2 * y + a[1], 2 * z + b[1], core, 2 * x + d[1])
                            for a in low
                            for b in low
                            for d in low
                        ]
                    )
    return groups


def exchange(blocks, groups):
    return lax.all_to_all(blocks, AXES, 0, 0, axis_index_groups=groups)


def swap_cores(block):
    count = lax.axis_size("seq")
    return lax.ppermute(block, "seq", [(i, i ^ 1) for i in range(count)])


def gather_far(w_block):
    far = exchange(jnp.broadcast_to(w_block, (32,) + w_block.shape), far_groups())
    return far.reshape(32 * w_block.shape[0], w_block.shape[1])


def gather_near(far):
    own = exchange(jnp.broadcast_to(far, (8,) + far.shape), near_groups())
    return own.reshape(8 * far.shape[0], far.shape[1])


def by_holder(x_local):
    tokens, width = x_local.shape
    rows = width // 512
    split = x_local.T.reshape(4, 2, 4, 2, 2, 2, 2, rows, tokens)
    return split.transpose(4, 1, 3, 6, 0, 2, 5, 7, 8).reshape(2, 256 * rows, tokens)


def in_order(first, second):
    rows, width = first.shape[0] // 256, first.shape[1]
    both = jnp.stack([first, second]).reshape(2, 2, 2, 2, 4, 4, 2, rows, width)
    return both.transpose(4, 1, 5, 2, 0, 6, 3, 7, 8).reshape(512 * rows, width)


def scatter_total(total):
    rows, width = total.shape[0] // 256, total.shape[1]
    total = exchange(total.reshape(8, 32 * rows, width), near_groups())
    total = jnp.sum(total.astype(jnp.float32), axis=0)
    total = total.astype(jnp.bfloat16).reshape(32, rows, width)
    return jnp.sum(exchange(total, far_groups()).astype(jnp.float32), axis=0)


def dot32(a, b):
    return jnp.dot(a, b, preferred_element_type=jnp.float32)


def body(layer_inputs, doc_start, w_qkv, d_context):
    x_local = layer_inputs[0]
    tok_rows = x_local.shape[0]
    q_width = d_context.shape[2]
    head_dim = (w_qkv.shape[1] - q_width) // 2
    heads = q_width // head_dim
    out_grad = d_context[0].reshape(tok_rows, heads, head_dim)
    doc_first = doc_start[0]
    positions = lax.axis_index("seq") * tok_rows + jnp.arange(tok_rows, dtype=jnp.int32)
    core = lax.axis_index("seq") & 1
    x_rows = by_holder(x_local)
    rows_own = lax.dynamic_index_in_dim(x_rows, core, 0, keepdims=False)
    rows_other = lax.dynamic_index_in_dim(x_rows, 1 - core, 0, keepdims=False)
    far = gather_far(w_qkv)
    rows_own, rows_other, far = lax.optimization_barrier((rows_own, rows_other, far))
    x_own, x_other = rows_own.T, rows_other.T
    w_own = gather_near(far)
    w_other = swap_cores(w_own)
    projected = dot32(x_own, w_own) + dot32(x_other, w_other)
    projected = projected.astype(jnp.bfloat16)
    queries = projected[:, :q_width].reshape(tok_rows, heads, head_dim)
    key_value = projected[:, q_width:]
    prior = from_behind(key_value, "seq", 1)
    key_rows = jnp.concatenate([prior[:, :head_dim], key_value[:, :head_dim]], axis=0)
    value_rows = jnp.concatenate([prior[:, head_dim:], key_value[:, head_dim:]], axis=0)
    key_pos = jnp.concatenate([positions - tok_rows, positions])
    grad_query, grad_keys, grad_values, log_total, row_dot = local_pass(
        queries, key_rows, value_rows, out_grad, doc_first, positions, key_pos
    )
    returned = from_behind(
        jnp.concatenate([grad_keys[:tok_rows], grad_values[:tok_rows]], axis=1).astype(
            jnp.bfloat16
        ),
        "seq",
        -1,
    ).astype(jnp.float32)
    far_keys = returned[:, :head_dim]
    far_values = returned[:, head_dim:]
    key_grad = (grad_keys[tok_rows:] + far_keys).astype(jnp.bfloat16)
    value_grad = (grad_values[tok_rows:] + far_values).astype(jnp.bfloat16)
    grad_proj = jnp.concatenate(
        [grad_query.astype(jnp.bfloat16).reshape(tok_rows, q_width), key_grad, value_grad], axis=1
    )
    received = swap_cores(dot32(rows_other, grad_proj).astype(jnp.bfloat16))
    total = dot32(rows_own, grad_proj) + received.astype(jnp.float32)
    weight_grad = scatter_total(total.astype(jnp.bfloat16))
    full_weights = in_order(
        jnp.where(core == 0, w_own, w_other), jnp.where(core == 0, w_other, w_own)
    )
    input_grad = lax.dot_general(
        grad_proj, full_weights, (((1,), (1,)), ((), ())), preferred_element_type=jnp.float32
    )
    input_grad = input_grad.astype(jnp.bfloat16).reshape(1, tok_rows, x_local.shape[1])
    return (input_grad, weight_grad)


def solution(mesh):
    return jax.shard_map(
        body,
        mesh=mesh,
        in_specs=(
            P("dp", "seq", None),
            P("dp", "seq"),
            P(("seq", "dp"), None),
            P("dp", "seq", None),
        ),
        out_specs=(P("dp", "seq", None), P(("seq", "dp"), None)),
        check_vma=False,
    )
```

```python
import jax
import jax.numpy as jnp
from jax import lax
from jax.experimental.layout import Layout, with_layout_constraint
from jax.sharding import PartitionSpec as P

WIN = 256


def from_behind(block, axis, distance):
    devices = range(lax.axis_size(axis))
    route = [(i - distance, i) for i in devices if i - distance in devices]
    return lax.ppermute(block, axis, route)


def masked_scores(queries, key_rows, doc_first, query_pos, key_pos):
    inv_root = queries.shape[2] ** (-0.5)
    scores = (
        jnp.einsum("rhd,kd->hrk", queries, key_rows, preferred_element_type=jnp.float32) * inv_root
    )
    visible = (
        (key_pos[None, :] <= query_pos[:, None])
        & (key_pos[None, :] > query_pos[:, None] - WIN)
        & (key_pos[None, :] >= doc_first[:, None])
    )
    return jnp.where(visible[None, :, :], scores, -jnp.inf)


def backward_terms(queries, key_rows, value_rows, out_grad, attn_probs, prob_low, row_dot):
    inv_root = queries.shape[2] ** (-0.5)
    prob_grad = jnp.einsum("rhd,kd->hrk", out_grad, value_rows, preferred_element_type=jnp.float32)
    score_grad = (attn_probs * (prob_grad - row_dot[:, :, None])).astype(jnp.bfloat16)
    grad_query = (
        jnp.einsum("hrk,kd->rhd", score_grad, key_rows, preferred_element_type=jnp.float32)
        * inv_root
    )
    grad_keys = (
        jnp.einsum("hrk,rhd->kd", score_grad, queries, preferred_element_type=jnp.float32)
        * inv_root
    )
    grad_values = jnp.einsum("hrk,rhd->kd", prob_low, out_grad, preferred_element_type=jnp.float32)
    return (grad_query, grad_keys, grad_values)


def local_pass(queries, key_rows, value_rows, out_grad, doc_first, query_pos, key_pos):
    scores = masked_scores(queries, key_rows, doc_first, query_pos, key_pos)
    row_max = jnp.max(scores, axis=2)
    log_total = row_max + jnp.log(jnp.sum(jnp.exp(scores - row_max[:, :, None]), axis=2))
    attn_probs = jnp.exp(scores - log_total[:, :, None])
    prob_low = attn_probs.astype(jnp.bfloat16)
    context = jnp.einsum("hrk,kd->rhd", prob_low, value_rows, preferred_element_type=jnp.float32)
    row_dot = jnp.sum(out_grad.astype(jnp.float32) * context, axis=2).T
    grad_query, grad_keys, grad_values = backward_terms(
        queries, key_rows, value_rows, out_grad, attn_probs, prob_low, row_dot
    )
    return (grad_query, grad_keys, grad_values, log_total, row_dot)


AXES = ("seq", "dp")


def spot(y, z, core, x):
    return ((y % 8 * 8 + z % 8) * 2 + core) * 4 + x % 4


def far_groups():
    return [
        [spot(2 * y + a, 2 * z + b, core, 2 * x + d) for y in range(4) for z in range(4) for x in range(2)]
        for a in range(2)
        for b in range(2)
        for core in range(2)
        for d in range(2)
    ]


def near_groups():
    groups = []
    for core in range(2):
        for y in range(4):
            for z in range(4):
                for x in range(2):
                    low = [(k, k) if core == 0 else (k, 2 - k) for k in range(2)]
                    groups.append(
                        [
                            spot(2 * y + a[1], 2 * z + b[1], core, 2 * x + d[1])
                            for a in low
                            for b in low
                            for d in low
                        ]
                    )
    return groups


def exchange(blocks, groups):
    return lax.all_to_all(blocks, AXES, 0, 0, axis_index_groups=groups)


def swap_cores(block):
    count = lax.axis_size("seq")
    return lax.ppermute(block, "seq", [(i, i ^ 1) for i in range(count)])


def gather_far(w_block):
    far = exchange(jnp.broadcast_to(w_block, (32,) + w_block.shape), far_groups())
    return far.reshape(32 * w_block.shape[0], w_block.shape[1])


def gather_near(far):
    own = exchange(jnp.broadcast_to(far, (8,) + far.shape), near_groups())
    return own.reshape(8 * far.shape[0], far.shape[1])


def by_holder(x_local):
    tokens, width = x_local.shape
    rows = width // 512
    split = x_local.T.reshape(4, 2, 4, 2, 2, 2, 2, rows, tokens)
    return split.transpose(4, 1, 3, 6, 0, 2, 5, 7, 8).reshape(2, 256 * rows, tokens)


def in_order(first, second):
    rows, width = first.shape[0] // 256, first.shape[1]
    both = jnp.stack([first, second]).reshape(2, 2, 2, 2, 4, 4, 2, rows, width)
    return both.transpose(4, 1, 5, 2, 0, 6, 3, 7, 8).reshape(512 * rows, width)


def scatter_total(total):
    rows, width = total.shape[0] // 256, total.shape[1]
    total = exchange(total.reshape(8, 32 * rows, width), near_groups())
    total = jnp.sum(total.astype(jnp.float32), axis=0)
    total = total.astype(jnp.bfloat16).reshape(32, rows, width)
    return jnp.sum(exchange(total, far_groups()).astype(jnp.float32), axis=0)


def core_pair(rows, core):
    own = lax.dynamic_index_in_dim(rows, core, 0, keepdims=False)
    return own, lax.dynamic_index_in_dim(rows, 1 - core, 0, keepdims=False)


def contract_rows(a, b):
    return lax.dot_general(
        a, b, (((0,), (0,)), ((), ())), preferred_element_type=jnp.float32
    )


def dot32(a, b):
    return jnp.dot(a, b, preferred_element_type=jnp.float32)


def body(layer_inputs, doc_start, w_qkv, d_context):
    x_local = layer_inputs[0]
    tok_rows = x_local.shape[0]
    q_width = d_context.shape[2]
    head_dim = (w_qkv.shape[1] - q_width) // 2
    heads = q_width // head_dim
    out_grad = d_context[0].reshape(tok_rows, heads, head_dim)
    doc_first = doc_start[0]
    positions = lax.axis_index("seq") * tok_rows + jnp.arange(tok_rows, dtype=jnp.int32)
    core = lax.axis_index("seq") & 1
    x_prior = with_layout_constraint(from_behind(x_local, "seq", 1), Layout((0, 1)))
    far = gather_far(w_qkv)
    own_pair, x_prior, far = lax.optimization_barrier(
        (core_pair(by_holder(x_local), core), x_prior, far)
    )
    w_own = gather_near(far)
    prior_pair = core_pair(by_holder(x_prior), core)
    rows_own, rows_other = (
        jnp.concatenate([a, b], axis=1) for a, b in zip(prior_pair, own_pair)
    )
    rows_own, rows_other, w_own = lax.optimization_barrier((rows_own, rows_other, w_own))
    w_other = swap_cores(w_own)
    projected = contract_rows(rows_own, w_own) + contract_rows(rows_other, w_other)
    projected = projected.astype(jnp.bfloat16)
    queries = projected[tok_rows:, :q_width].reshape(tok_rows, heads, head_dim)
    key_rows = projected[:, q_width : q_width + head_dim]
    value_rows = projected[:, q_width + head_dim :]
    key_pos = jnp.concatenate([positions - tok_rows, positions])
    grad_query, grad_keys, grad_values, log_total, row_dot = local_pass(
        queries, key_rows, value_rows, out_grad, doc_first, positions, key_pos
    )
    low_query = grad_query.astype(jnp.bfloat16).reshape(tok_rows, q_width)
    grad_kv = jnp.concatenate([grad_keys, grad_values], axis=1)
    low_kv = grad_kv.astype(jnp.bfloat16)
    low_all = jnp.concatenate(
        [jnp.concatenate([jnp.zeros_like(low_query), low_query], axis=0), low_kv], axis=1
    )
    sent = dot32(rows_other, low_all).astype(jnp.bfloat16)
    sent, far_kv = lax.optimization_barrier((sent, low_kv[:tok_rows]))
    received = swap_cores(sent)
    returned = from_behind(far_kv, "seq", -1).astype(jnp.float32)
    total = dot32(rows_own, low_all) + received.astype(jnp.float32)
    weight_grad = scatter_total(total.astype(jnp.bfloat16))
    grad_proj = jnp.concatenate(
        [low_query, (grad_kv[tok_rows:] + returned).astype(jnp.bfloat16)], axis=1
    )
    full_weights = in_order(
        jnp.where(core == 0, w_own, w_other), jnp.where(core == 0, w_other, w_own)
    )
    input_grad = lax.dot_general(
        grad_proj, full_weights, (((1,), (1,)), ((), ())), preferred_element_type=jnp.float32
    )
    input_grad = input_grad.astype(jnp.bfloat16).reshape(1, tok_rows, x_local.shape[1])
    return (input_grad, weight_grad)


def solution(mesh):
    return jax.shard_map(
        body,
        mesh=mesh,
        in_specs=(
            P("dp", "seq", None),
            P("dp", "seq"),
            P(("seq", "dp"), None),
            P("dp", "seq", None),
        ),
        out_specs=(P("dp", "seq", None), P(("seq", "dp"), None)),
        check_vma=False,
    )
```

```python
import jax
import jax.numpy as jnp
from jax import lax
from jax.experimental.layout import Layout, with_layout_constraint
from jax.sharding import PartitionSpec as P

WIN = 256


def from_behind(block, axis, distance):
    devices = range(lax.axis_size(axis))
    route = [(i - distance, i) for i in devices if i - distance in devices]
    return lax.ppermute(block, axis, route)


def from_behind_rows(rows):
    return with_layout_constraint(from_behind(rows, "seq", 1), Layout((0, 1)))


def masked_scores(queries, key_rows, doc_first, query_pos, key_pos):
    inv_root = queries.shape[2] ** (-0.5)
    scores = (
        jnp.einsum("rhd,kd->hrk", queries, key_rows, preferred_element_type=jnp.float32) * inv_root
    )
    visible = (
        (key_pos[None, :] <= query_pos[:, None])
        & (key_pos[None, :] > query_pos[:, None] - WIN)
        & (key_pos[None, :] >= doc_first[:, None])
    )
    return jnp.where(visible[None, :, :], scores, -jnp.inf)


def backward_terms(queries, key_rows, value_rows, out_grad, attn_probs, prob_low, row_dot):
    inv_root = queries.shape[2] ** (-0.5)
    prob_grad = jnp.einsum("rhd,kd->hrk", out_grad, value_rows, preferred_element_type=jnp.float32)
    score_grad = (attn_probs * (prob_grad - row_dot[:, :, None])).astype(jnp.bfloat16)
    grad_query = (
        jnp.einsum("hrk,kd->rhd", score_grad, key_rows, preferred_element_type=jnp.float32)
        * inv_root
    )
    grad_keys = (
        jnp.einsum("hrk,rhd->kd", score_grad, queries, preferred_element_type=jnp.float32)
        * inv_root
    )
    grad_values = jnp.einsum("hrk,rhd->kd", prob_low, out_grad, preferred_element_type=jnp.float32)
    return (grad_query, grad_keys, grad_values)


def local_pass(queries, key_rows, value_rows, out_grad, doc_first, query_pos, key_pos):
    scores = masked_scores(queries, key_rows, doc_first, query_pos, key_pos)
    row_max = jnp.max(scores, axis=2)
    log_total = row_max + jnp.log(jnp.sum(jnp.exp(scores - row_max[:, :, None]), axis=2))
    attn_probs = jnp.exp(scores - log_total[:, :, None])
    prob_low = attn_probs.astype(jnp.bfloat16)
    context = jnp.einsum("hrk,kd->rhd", prob_low, value_rows, preferred_element_type=jnp.float32)
    row_dot = jnp.sum(out_grad.astype(jnp.float32) * context, axis=2).T
    grad_query, grad_keys, grad_values = backward_terms(
        queries, key_rows, value_rows, out_grad, attn_probs, prob_low, row_dot
    )
    return (grad_query, grad_keys, grad_values, log_total, row_dot)


AXES = ("seq", "dp")


def spot(y, z, core, x):
    return ((y % 8 * 8 + z % 8) * 2 + core) * 4 + x % 4


def far_groups():
    return [
        [spot(2 * y + a, 2 * z + b, core, 2 * x + d) for y in range(4) for z in range(4) for x in range(2)]
        for a in range(2)
        for b in range(2)
        for core in range(2)
        for d in range(2)
    ]


def near_groups():
    groups = []
    for core in range(2):
        for y in range(4):
            for z in range(4):
                for x in range(2):
                    low = [(k, k) if core == 0 else (k, 2 - k) for k in range(2)]
                    groups.append(
                        [
                            spot(2 * y + a[1], 2 * z + b[1], core, 2 * x + d[1])
                            for a in low
                            for b in low
                            for d in low
                        ]
                    )
    return groups


def exchange(blocks, groups):
    return lax.all_to_all(blocks, AXES, 0, 0, axis_index_groups=groups)


def swap_cores(block):
    count = lax.axis_size("seq")
    return lax.ppermute(block, "seq", [(i, i ^ 1) for i in range(count)])


def gather_far(w_block):
    far = exchange(jnp.broadcast_to(w_block, (32,) + w_block.shape), far_groups())
    return far.reshape(32 * w_block.shape[0], w_block.shape[1])


def gather_near(far):
    own = exchange(jnp.broadcast_to(far, (8,) + far.shape), near_groups())
    return own.reshape(8 * far.shape[0], far.shape[1])


def by_holder(x_local):
    tokens, width = x_local.shape
    rows = width // 512
    split = x_local.T.reshape(4, 2, 4, 2, 2, 2, 2, rows, tokens)
    return split.transpose(4, 1, 3, 6, 0, 2, 5, 7, 8).reshape(2, 256 * rows, tokens)


def in_order(first, second):
    rows, width = first.shape[0] // 256, first.shape[1]
    both = jnp.stack([first, second]).reshape(2, 2, 2, 2, 4, 4, 2, rows, width)
    return both.transpose(4, 1, 5, 2, 0, 6, 3, 7, 8).reshape(512 * rows, width)


def scatter_total(total):
    rows, width = total.shape[0] // 256, total.shape[1]
    total = exchange(total.reshape(8, 32 * rows, width), near_groups())
    total = jnp.sum(total.astype(jnp.float32), axis=0)
    total = total.astype(jnp.bfloat16).reshape(32, rows, width)
    return jnp.sum(exchange(total, far_groups()).astype(jnp.float32), axis=0)


def core_pair(rows, core):
    own = lax.dynamic_index_in_dim(rows, core, 0, keepdims=False)
    return own, lax.dynamic_index_in_dim(rows, 1 - core, 0, keepdims=False)


def contract_rows(a, b):
    return lax.dot_general(
        a, b, (((0,), (0,)), ((), ())), preferred_element_type=jnp.float32
    )


def dot32(a, b):
    return jnp.dot(a, b, preferred_element_type=jnp.float32)


def body(layer_inputs, doc_start, w_qkv, d_context):
    x_local = layer_inputs[0]
    tok_rows = x_local.shape[0]
    q_width = d_context.shape[2]
    head_dim = (w_qkv.shape[1] - q_width) // 2
    heads = q_width // head_dim
    out_grad = d_context[0].reshape(tok_rows, heads, head_dim)
    doc_first = doc_start[0]
    positions = lax.axis_index("seq") * tok_rows + jnp.arange(tok_rows, dtype=jnp.int32)
    core = lax.axis_index("seq") & 1
    half = tok_rows // 2
    prior_first = from_behind_rows(x_local[:half])
    far = gather_far(w_qkv)
    own_pair, prior_first, far = lax.optimization_barrier(
        (core_pair(by_holder(x_local), core), prior_first, far)
    )
    prior_second = from_behind_rows(x_local[half:])
    w_own = gather_near(far)
    first_pair = core_pair(by_holder(prior_first), core)
    second_pair = core_pair(by_holder(prior_second), core)
    rows_own, rows_other = (
        jnp.concatenate(parts, axis=1) for parts in zip(first_pair, second_pair, own_pair)
    )
    rows_own, rows_other, w_own = lax.optimization_barrier((rows_own, rows_other, w_own))
    w_other = swap_cores(w_own)
    projected = contract_rows(rows_own, w_own) + contract_rows(rows_other, w_other)
    projected = projected.astype(jnp.bfloat16)
    queries = projected[tok_rows:, :q_width].reshape(tok_rows, heads, head_dim)
    key_rows = projected[:, q_width : q_width + head_dim]
    value_rows = projected[:, q_width + head_dim :]
    key_pos = jnp.concatenate([positions - tok_rows, positions])
    grad_query, grad_keys, grad_values, log_total, row_dot = local_pass(
        queries, key_rows, value_rows, out_grad, doc_first, positions, key_pos
    )
    low_query = grad_query.astype(jnp.bfloat16).reshape(tok_rows, q_width)
    grad_kv = jnp.concatenate([grad_keys, grad_values], axis=1)
    low_kv = grad_kv.astype(jnp.bfloat16)
    low_all = jnp.concatenate(
        [jnp.concatenate([jnp.zeros_like(low_query), low_query], axis=0), low_kv], axis=1
    )
    sent = dot32(rows_other, low_all).astype(jnp.bfloat16)
    sent, far_kv = lax.optimization_barrier((sent, low_kv[:tok_rows]))
    received = swap_cores(sent)
    returned = from_behind(far_kv, "seq", -1).astype(jnp.float32)
    total = dot32(rows_own, low_all) + received.astype(jnp.float32)
    weight_grad = scatter_total(total.astype(jnp.bfloat16))
    grad_proj = jnp.concatenate(
        [low_query, (grad_kv[tok_rows:] + returned).astype(jnp.bfloat16)], axis=1
    )
    full_weights = in_order(
        jnp.where(core == 0, w_own, w_other), jnp.where(core == 0, w_other, w_own)
    )
    input_grad = lax.dot_general(
        grad_proj, full_weights, (((1,), (1,)), ((), ())), preferred_element_type=jnp.float32
    )
    input_grad = input_grad.astype(jnp.bfloat16).reshape(1, tok_rows, x_local.shape[1])
    return (input_grad, weight_grad)


def solution(mesh):
    return jax.shard_map(
        body,
        mesh=mesh,
        in_specs=(
            P("dp", "seq", None),
            P("dp", "seq"),
            P(("seq", "dp"), None),
            P("dp", "seq", None),
        ),
        out_specs=(P("dp", "seq", None), P(("seq", "dp"), None)),
        check_vma=False,
    )
```

```python
import jax
import jax.numpy as jnp
from jax import lax
from jax.experimental.layout import Layout, with_layout_constraint
from jax.sharding import PartitionSpec as P

WIN = 256


def from_behind(block, axis, distance):
    devices = range(lax.axis_size(axis))
    route = [(i - distance, i) for i in devices if i - distance in devices]
    return lax.ppermute(block, axis, route)


def masked_scores(queries, key_rows, doc_first, query_pos, key_pos):
    inv_root = queries.shape[2] ** (-0.5)
    scores = (
        jnp.einsum("rhd,kd->hrk", queries, key_rows, preferred_element_type=jnp.float32) * inv_root
    )
    visible = (
        (key_pos[None, :] <= query_pos[:, None])
        & (key_pos[None, :] > query_pos[:, None] - WIN)
        & (key_pos[None, :] >= doc_first[:, None])
    )
    return jnp.where(visible[None, :, :], scores, -jnp.inf)


def backward_terms(queries, key_rows, value_rows, out_grad, attn_probs, prob_low, row_dot):
    inv_root = queries.shape[2] ** (-0.5)
    prob_grad = jnp.einsum("rhd,kd->hrk", out_grad, value_rows, preferred_element_type=jnp.float32)
    score_grad = (attn_probs * (prob_grad - row_dot[:, :, None])).astype(jnp.bfloat16)
    grad_query = (
        jnp.einsum("hrk,kd->rhd", score_grad, key_rows, preferred_element_type=jnp.float32)
        * inv_root
    )
    grad_keys = (
        jnp.einsum("hrk,rhd->kd", score_grad, queries, preferred_element_type=jnp.float32)
        * inv_root
    )
    grad_values = jnp.einsum("hrk,rhd->kd", prob_low, out_grad, preferred_element_type=jnp.float32)
    return (grad_query, grad_keys, grad_values)


def local_pass(queries, key_rows, value_rows, out_grad, doc_first, query_pos, key_pos):
    scores = masked_scores(queries, key_rows, doc_first, query_pos, key_pos)
    row_max = jnp.max(scores, axis=2)
    log_total = row_max + jnp.log(jnp.sum(jnp.exp(scores - row_max[:, :, None]), axis=2))
    attn_probs = jnp.exp(scores - log_total[:, :, None])
    prob_low = attn_probs.astype(jnp.bfloat16)
    context = jnp.einsum("hrk,kd->rhd", prob_low, value_rows, preferred_element_type=jnp.float32)
    row_dot = jnp.sum(out_grad.astype(jnp.float32) * context, axis=2).T
    grad_query, grad_keys, grad_values = backward_terms(
        queries, key_rows, value_rows, out_grad, attn_probs, prob_low, row_dot
    )
    return (grad_query, grad_keys, grad_values, log_total, row_dot)


AXES = ("seq", "dp")


def spot(y, z, core, x):
    return ((y % 8 * 8 + z % 8) * 2 + core) * 4 + x % 4


def far_groups():
    return [
        [spot(2 * y + a, 2 * z + b, core, 2 * x + d) for y in range(4) for z in range(4) for x in range(2)]
        for a in range(2)
        for b in range(2)
        for core in range(2)
        for d in range(2)
    ]


def near_groups():
    groups = []
    for core in range(2):
        for y in range(4):
            for z in range(4):
                for x in range(2):
                    low = [(k, k) if core == 0 else (k, 2 - k) for k in range(2)]
                    groups.append(
                        [
                            spot(2 * y + a[1], 2 * z + b[1], core, 2 * x + d[1])
                            for a in low
                            for b in low
                            for d in low
                        ]
                    )
    return groups


def exchange(blocks, groups):
    return lax.all_to_all(blocks, AXES, 0, 0, axis_index_groups=groups)


def swap_cores(block):
    count = lax.axis_size("seq")
    return lax.ppermute(block, "seq", [(i, i ^ 1) for i in range(count)])


def gather_far(w_block):
    far = exchange(jnp.broadcast_to(w_block, (32,) + w_block.shape), far_groups())
    return far.reshape(32 * w_block.shape[0], w_block.shape[1])


def gather_near(far):
    own = exchange(jnp.broadcast_to(far, (8,) + far.shape), near_groups())
    return own.reshape(8 * far.shape[0], far.shape[1])


def by_holder(x_local):
    tokens, width = x_local.shape
    rows = width // 512
    split = x_local.T.reshape(4, 2, 4, 2, 2, 2, 2, rows, tokens)
    return split.transpose(4, 1, 3, 6, 0, 2, 5, 7, 8).reshape(2, 256 * rows, tokens)


def in_order(first, second):
    rows, width = first.shape[0] // 256, first.shape[1]
    both = jnp.stack([first, second]).reshape(2, 2, 2, 2, 4, 4, 2, rows, width)
    return both.transpose(4, 1, 5, 2, 0, 6, 3, 7, 8).reshape(512 * rows, width)


def scatter_total(total):
    rows, width = total.shape[0] // 256, total.shape[1]
    total = exchange(total.reshape(8, 32 * rows, width), near_groups())
    total = jnp.sum(total.astype(jnp.float32), axis=0)
    total = total.astype(jnp.bfloat16).reshape(32, rows, width)
    return jnp.sum(exchange(total, far_groups()).astype(jnp.float32), axis=0)


def core_pair(rows, core):
    own = lax.dynamic_index_in_dim(rows, core, 0, keepdims=False)
    return own, lax.dynamic_index_in_dim(rows, 1 - core, 0, keepdims=False)


def contract_rows(a, b):
    return lax.dot_general(
        a, b, (((0,), (0,)), ((), ())), preferred_element_type=jnp.float32
    )


def dot32(a, b):
    return jnp.dot(a, b, preferred_element_type=jnp.float32)


def body(layer_inputs, doc_start, w_qkv, d_context):
    x_local = layer_inputs[0]
    tok_rows = x_local.shape[0]
    q_width = d_context.shape[2]
    head_dim = (w_qkv.shape[1] - q_width) // 2
    heads = q_width // head_dim
    out_grad = d_context[0].reshape(tok_rows, heads, head_dim)
    doc_first = doc_start[0]
    positions = lax.axis_index("seq") * tok_rows + jnp.arange(tok_rows, dtype=jnp.int32)
    core = lax.axis_index("seq") & 1
    seq_count = lax.axis_size("seq")
    chip_pairs = [[i, (i + 1) % seq_count] for i in range(1, seq_count, 2)]
    x_before = lax.all_gather(x_local, "seq", axis_index_groups=chip_pairs)[0]
    x_partner = with_layout_constraint(swap_cores(x_local), Layout((0, 1)))
    far = gather_far(w_qkv)
    own_pair, x_partner, far = lax.optimization_barrier(
        (core_pair(by_holder(x_local), core), x_partner, far)
    )
    w_own = gather_near(far)
    x_prior = jnp.where(core == 0, x_before, x_partner)
    prior_pair = core_pair(by_holder(x_prior), core)
    rows_own, rows_other = (
        jnp.concatenate([a, b], axis=1) for a, b in zip(prior_pair, own_pair)
    )
    rows_own, rows_other, w_own = lax.optimization_barrier((rows_own, rows_other, w_own))
    w_other = swap_cores(w_own)
    projected = contract_rows(rows_own, w_own) + contract_rows(rows_other, w_other)
    projected = projected.astype(jnp.bfloat16)
    queries = projected[tok_rows:, :q_width].reshape(tok_rows, heads, head_dim)
    key_rows = projected[:, q_width : q_width + head_dim]
    value_rows = projected[:, q_width + head_dim :]
    key_pos = jnp.concatenate([positions - tok_rows, positions])
    grad_query, grad_keys, grad_values, log_total, row_dot = local_pass(
        queries, key_rows, value_rows, out_grad, doc_first, positions, key_pos
    )
    low_query = grad_query.astype(jnp.bfloat16).reshape(tok_rows, q_width)
    grad_kv = jnp.concatenate([grad_keys, grad_values], axis=1)
    low_kv = grad_kv.astype(jnp.bfloat16)
    low_all = jnp.concatenate(
        [jnp.concatenate([jnp.zeros_like(low_query), low_query], axis=0), low_kv], axis=1
    )
    sent = dot32(rows_other, low_all).astype(jnp.bfloat16)
    sent, far_kv = lax.optimization_barrier((sent, low_kv[:tok_rows]))
    received = swap_cores(sent)
    returned = from_behind(far_kv, "seq", -1).astype(jnp.float32)
    total = dot32(rows_own, low_all) + received.astype(jnp.float32)
    weight_grad = scatter_total(total.astype(jnp.bfloat16))
    grad_proj = jnp.concatenate(
        [low_query, (grad_kv[tok_rows:] + returned).astype(jnp.bfloat16)], axis=1
    )
    full_weights = in_order(
        jnp.where(core == 0, w_own, w_other), jnp.where(core == 0, w_other, w_own)
    )
    input_grad = lax.dot_general(
        grad_proj, full_weights, (((1,), (1,)), ((), ())), preferred_element_type=jnp.float32
    )
    input_grad = input_grad.astype(jnp.bfloat16).reshape(1, tok_rows, x_local.shape[1])
    return (input_grad, weight_grad)


def solution(mesh):
    return jax.shard_map(
        body,
        mesh=mesh,
        in_specs=(
            P("dp", "seq", None),
            P("dp", "seq"),
            P(("seq", "dp"), None),
            P("dp", "seq", None),
        ),
        out_specs=(P("dp", "seq", None), P(("seq", "dp"), None)),
        check_vma=False,
    )
```

```python
import jax
import jax.numpy as jnp
from jax import lax
from jax.experimental.layout import Layout, with_layout_constraint
from jax.sharding import PartitionSpec as P

WIN = 256


def from_behind(block, axis, distance):
    devices = range(lax.axis_size(axis))
    route = [(i - distance, i) for i in devices if i - distance in devices]
    return lax.ppermute(block, axis, route)


def masked_scores(queries, key_rows, doc_first, query_pos, key_pos):
    inv_root = queries.shape[2] ** (-0.5)
    scores = (
        jnp.einsum("rhd,kd->hrk", queries, key_rows, preferred_element_type=jnp.float32) * inv_root
    )
    visible = (
        (key_pos[None, :] <= query_pos[:, None])
        & (key_pos[None, :] > query_pos[:, None] - WIN)
        & (key_pos[None, :] >= doc_first[:, None])
    )
    return jnp.where(visible[None, :, :], scores, -jnp.inf)


def backward_terms(queries, key_rows, value_rows, out_grad, attn_probs, prob_low, row_dot):
    inv_root = queries.shape[2] ** (-0.5)
    prob_grad = jnp.einsum("rhd,kd->hrk", out_grad, value_rows, preferred_element_type=jnp.float32)
    score_grad = (attn_probs * (prob_grad - row_dot[:, :, None])).astype(jnp.bfloat16)
    grad_query = (
        jnp.einsum("hrk,kd->rhd", score_grad, key_rows, preferred_element_type=jnp.float32)
        * inv_root
    )
    grad_keys = (
        jnp.einsum("hrk,rhd->kd", score_grad, queries, preferred_element_type=jnp.float32)
        * inv_root
    )
    grad_values = jnp.einsum("hrk,rhd->kd", prob_low, out_grad, preferred_element_type=jnp.float32)
    return (grad_query, grad_keys, grad_values)


def local_pass(queries, key_rows, value_rows, out_grad, doc_first, query_pos, key_pos):
    scores = masked_scores(queries, key_rows, doc_first, query_pos, key_pos)
    row_max = jnp.max(scores, axis=2)
    log_total = row_max + jnp.log(jnp.sum(jnp.exp(scores - row_max[:, :, None]), axis=2))
    attn_probs = jnp.exp(scores - log_total[:, :, None])
    prob_low = attn_probs.astype(jnp.bfloat16)
    context = jnp.einsum("hrk,kd->rhd", prob_low, value_rows, preferred_element_type=jnp.float32)
    row_dot = jnp.sum(out_grad.astype(jnp.float32) * context, axis=2).T
    grad_query, grad_keys, grad_values = backward_terms(
        queries, key_rows, value_rows, out_grad, attn_probs, prob_low, row_dot
    )
    return (grad_query, grad_keys, grad_values, log_total, row_dot)


AXES = ("seq", "dp")


def spot(y, z, core, x):
    return ((y % 8 * 8 + z % 8) * 2 + core) * 4 + x % 4


def far_groups():
    return [
        [spot(2 * y + a, 2 * z + b, core, 2 * x + d) for y in range(4) for z in range(4) for x in range(2)]
        for a in range(2)
        for b in range(2)
        for core in range(2)
        for d in range(2)
    ]


def near_groups():
    groups = []
    for core in range(2):
        for y in range(4):
            for z in range(4):
                for x in range(2):
                    low = [(k, k) if core == 0 else (k, 2 - k) for k in range(2)]
                    groups.append(
                        [
                            spot(2 * y + a[1], 2 * z + b[1], core, 2 * x + d[1])
                            for a in low
                            for b in low
                            for d in low
                        ]
                    )
    return groups


def exchange(blocks, groups):
    return lax.all_to_all(blocks, AXES, 0, 0, axis_index_groups=groups)


def swap_cores(block):
    count = lax.axis_size("seq")
    return lax.ppermute(block, "seq", [(i, i ^ 1) for i in range(count)])


def gather_far(w_block):
    far = exchange(jnp.broadcast_to(w_block, (32,) + w_block.shape), far_groups())
    return far.reshape(32 * w_block.shape[0], w_block.shape[1])


def gather_near(far):
    own = exchange(jnp.broadcast_to(far, (8,) + far.shape), near_groups())
    return own.reshape(8 * far.shape[0], far.shape[1])


def by_holder(x_local):
    tokens, width = x_local.shape
    rows = width // 512
    split = x_local.T.reshape(4, 2, 4, 2, 2, 2, 2, rows, tokens)
    return split.transpose(4, 1, 3, 6, 0, 2, 5, 7, 8).reshape(2, 256 * rows, tokens)


def in_order(first, second):
    rows, width = first.shape[0] // 256, first.shape[1]
    both = jnp.stack([first, second]).reshape(2, 2, 2, 2, 4, 4, 2, rows, width)
    return both.transpose(4, 1, 5, 2, 0, 6, 3, 7, 8).reshape(512 * rows, width)


def scatter_total(total):
    rows, width = total.shape[0] // 256, total.shape[1]
    total = exchange(total.reshape(8, 32 * rows, width), near_groups())
    total = jnp.sum(total.astype(jnp.float32), axis=0)
    total = total.astype(jnp.bfloat16).reshape(32, rows, width)
    return jnp.sum(exchange(total, far_groups()).astype(jnp.float32), axis=0)


def half_rows(rows, core):
    return lax.dynamic_index_in_dim(rows, core, 0, keepdims=False)


def contract_rows(a, b):
    return lax.dot_general(
        a, b, (((0,), (0,)), ((), ())), preferred_element_type=jnp.float32
    )


def dot32(a, b):
    return jnp.dot(a, b, preferred_element_type=jnp.float32)


def body(layer_inputs, doc_start, w_qkv, d_context):
    x_local = layer_inputs[0]
    tok_rows = x_local.shape[0]
    q_width = d_context.shape[2]
    head_dim = (w_qkv.shape[1] - q_width) // 2
    heads = q_width // head_dim
    out_grad = d_context[0].reshape(tok_rows, heads, head_dim)
    doc_first = doc_start[0]
    positions = lax.axis_index("seq") * tok_rows + jnp.arange(tok_rows, dtype=jnp.int32)
    core = lax.axis_index("seq") & 1
    first = core == 0
    far = gather_far(w_qkv)
    x_partner = with_layout_constraint(swap_cores(x_local), Layout((0, 1)))
    rows_mine, x_partner, far = lax.optimization_barrier(
        (half_rows(by_holder(x_local), core), x_partner, far)
    )
    x_half = jnp.concatenate([rows_mine, half_rows(by_holder(x_partner), core)], axis=1)
    w_half = gather_near(far)
    x_half, w_half = lax.optimization_barrier((x_half, w_half))
    partial = contract_rows(x_half, w_half)
    mine, theirs = partial[:tok_rows], partial[tok_rows:]
    got = swap_cores(
        jnp.concatenate([theirs, mine[:, q_width:]], axis=1).astype(jnp.bfloat16)
    ).astype(jnp.float32)
    width = mine.shape[1]
    projected = (mine + got[:, :width]).astype(jnp.bfloat16)
    partner_kv = (theirs[:, q_width:] + got[:, width:]).astype(jnp.bfloat16)
    queries = projected[:, :q_width].reshape(tok_rows, heads, head_dim)
    key_value = projected[:, q_width:]
    seq_count = lax.axis_size("seq")
    before = lax.ppermute(key_value, "seq", [(i, i + 1) for i in range(1, seq_count - 1, 2)])
    prior = jnp.where(first, before, partner_kv)
    key_rows = jnp.concatenate([prior[:, :head_dim], key_value[:, :head_dim]], axis=0)
    value_rows = jnp.concatenate([prior[:, head_dim:], key_value[:, head_dim:]], axis=0)
    key_pos = jnp.concatenate([positions - tok_rows, positions])
    grad_query, grad_keys, grad_values, log_total, row_dot = local_pass(
        queries, key_rows, value_rows, out_grad, doc_first, positions, key_pos
    )
    low_query = grad_query.astype(jnp.bfloat16).reshape(tok_rows, q_width)
    grad_kv = jnp.concatenate([grad_keys, grad_values], axis=1)
    low_kv = grad_kv.astype(jnp.bfloat16)
    far_kv, own_kv = low_kv[:tok_rows], low_kv[tok_rows:]
    got = swap_cores(jnp.concatenate([low_query, own_kv, far_kv], axis=1))
    got_query, got_own = got[:, :q_width], got[:, q_width : 2 * q_width]
    got_far = got[:, 2 * q_width :]
    returned = from_behind(jnp.where(first, far_kv, got_far), "seq", -2)
    mine_far = jnp.where(first, got_far, returned).astype(jnp.float32)
    partner_far = jnp.where(first, returned, far_kv).astype(jnp.float32)
    grad_proj = jnp.concatenate(
        [low_query, (grad_kv[tok_rows:] + mine_far).astype(jnp.bfloat16)], axis=1
    )
    partner_proj = jnp.concatenate(
        [got_query, (got_own.astype(jnp.float32) + partner_far).astype(jnp.bfloat16)], axis=1
    )
    total = dot32(x_half, jnp.concatenate([grad_proj, partner_proj], axis=0))
    w_half, total = lax.optimization_barrier((w_half, total.astype(jnp.bfloat16)))
    weight_grad = scatter_total(total)
    w_rest = swap_cores(w_half)
    full_weights = in_order(
        jnp.where(first, w_half, w_rest), jnp.where(first, w_rest, w_half)
    )
    input_grad = lax.dot_general(
        grad_proj, full_weights, (((1,), (1,)), ((), ())), preferred_element_type=jnp.float32
    )
    input_grad = input_grad.astype(jnp.bfloat16).reshape(1, tok_rows, x_local.shape[1])
    return (input_grad, weight_grad)


def solution(mesh):
    return jax.shard_map(
        body,
        mesh=mesh,
        in_specs=(
            P("dp", "seq", None),
            P("dp", "seq"),
            P(("seq", "dp"), None),
            P("dp", "seq", None),
        ),
        out_specs=(P("dp", "seq", None), P(("seq", "dp"), None)),
        check_vma=False,
    )
```

```python
import jax
import jax.numpy as jnp
from jax import lax
from jax.sharding import PartitionSpec as P

WIN = 256


def from_behind(block, axis, distance):
    devices = range(lax.axis_size(axis))
    route = [(i - distance, i) for i in devices if i - distance in devices]
    return lax.ppermute(block, axis, route)


def masked_scores(queries, key_rows, doc_first, query_pos, key_pos):
    inv_root = queries.shape[2] ** (-0.5)
    scores = (
        jnp.einsum("rhd,kd->hrk", queries, key_rows, preferred_element_type=jnp.float32) * inv_root
    )
    visible = (
        (key_pos[None, :] <= query_pos[:, None])
        & (key_pos[None, :] > query_pos[:, None] - WIN)
        & (key_pos[None, :] >= doc_first[:, None])
    )
    return jnp.where(visible[None, :, :], scores, -jnp.inf)


def backward_terms(queries, key_rows, value_rows, out_grad, attn_probs, prob_low, row_dot):
    inv_root = queries.shape[2] ** (-0.5)
    prob_grad = jnp.einsum("rhd,kd->hrk", out_grad, value_rows, preferred_element_type=jnp.float32)
    score_grad = (attn_probs * (prob_grad - row_dot[:, :, None])).astype(jnp.bfloat16)
    grad_query = (
        jnp.einsum("hrk,kd->rhd", score_grad, key_rows, preferred_element_type=jnp.float32)
        * inv_root
    )
    grad_keys = (
        jnp.einsum("hrk,rhd->kd", score_grad, queries, preferred_element_type=jnp.float32)
        * inv_root
    )
    grad_values = jnp.einsum("hrk,rhd->kd", prob_low, out_grad, preferred_element_type=jnp.float32)
    return (grad_query, grad_keys, grad_values)


def local_pass(queries, key_rows, value_rows, out_grad, doc_first, query_pos, key_pos):
    scores = masked_scores(queries, key_rows, doc_first, query_pos, key_pos)
    row_max = jnp.max(scores, axis=2)
    log_total = row_max + jnp.log(jnp.sum(jnp.exp(scores - row_max[:, :, None]), axis=2))
    attn_probs = jnp.exp(scores - log_total[:, :, None])
    prob_low = attn_probs.astype(jnp.bfloat16)
    context = jnp.einsum("hrk,kd->rhd", prob_low, value_rows, preferred_element_type=jnp.float32)
    row_dot = jnp.sum(out_grad.astype(jnp.float32) * context, axis=2).T
    grad_query, grad_keys, grad_values = backward_terms(
        queries, key_rows, value_rows, out_grad, attn_probs, prob_low, row_dot
    )
    return (grad_query, grad_keys, grad_values, log_total, row_dot)


AXES = ("seq", "dp")


def spot(y, z, core, x):
    return ((y % 8 * 8 + z % 8) * 2 + core) * 4 + x % 4


def far_groups():
    return [
        [spot(2 * y + a, 2 * z + b, core, 2 * x + d) for y in range(4) for z in range(4) for x in range(2)]
        for a in range(2)
        for b in range(2)
        for core in range(2)
        for d in range(2)
    ]


def near_groups():
    groups = []
    for core in range(2):
        for y in range(4):
            for z in range(4):
                for x in range(2):
                    low = [(k, k) if core == 0 else (k, 2 - k) for k in range(2)]
                    groups.append(
                        [
                            spot(2 * y + a[1], 2 * z + b[1], core, 2 * x + d[1])
                            for a in low
                            for b in low
                            for d in low
                        ]
                    )
    return groups


def exchange(blocks, groups):
    return lax.all_to_all(blocks, AXES, 0, 0, axis_index_groups=groups)


def swap_cores(block):
    count = lax.axis_size("seq")
    return lax.ppermute(block, "seq", [(i, i ^ 1) for i in range(count)])


def gather_far(w_block):
    far = exchange(jnp.broadcast_to(w_block, (32,) + w_block.shape), far_groups())
    return far.reshape(32 * w_block.shape[0], w_block.shape[1])


def gather_near(far):
    own = exchange(jnp.broadcast_to(far, (8,) + far.shape), near_groups())
    return own.reshape(8 * far.shape[0], far.shape[1])


def by_holder(x_local):
    tokens, width = x_local.shape
    rows = width // 512
    split = x_local.T.reshape(4, 2, 4, 2, 2, 2, 2, rows, tokens)
    return split.transpose(4, 1, 3, 6, 0, 2, 5, 7, 8).reshape(2, 256 * rows, tokens)


def in_order(first, second):
    rows, width = first.shape[0] // 256, first.shape[1]
    both = jnp.stack([first, second]).reshape(2, 2, 2, 2, 4, 4, 2, rows, width)
    return both.transpose(4, 1, 5, 2, 0, 6, 3, 7, 8).reshape(512 * rows, width)


def scatter_total(total):
    rows, width = total.shape[0] // 256, total.shape[1]
    total = exchange(total.reshape(8, 32 * rows, width), near_groups())
    total = jnp.sum(total.astype(jnp.float32), axis=0)
    total = total.astype(jnp.bfloat16).reshape(32, rows, width)
    return jnp.sum(exchange(total, far_groups()).astype(jnp.float32), axis=0)


def dot32(a, b):
    return jnp.dot(a, b, preferred_element_type=jnp.float32)


def body(layer_inputs, doc_start, w_qkv, d_context):
    x_local = layer_inputs[0]
    tok_rows = x_local.shape[0]
    q_width = d_context.shape[2]
    head_dim = (w_qkv.shape[1] - q_width) // 2
    heads = q_width // head_dim
    out_grad = d_context[0].reshape(tok_rows, heads, head_dim)
    doc_first = doc_start[0]
    positions = lax.axis_index("seq") * tok_rows + jnp.arange(tok_rows, dtype=jnp.int32)
    core = lax.axis_index("seq") & 1
    x_rows = by_holder(x_local)
    rows_own = lax.dynamic_index_in_dim(x_rows, core, 0, keepdims=False)
    rows_other = lax.dynamic_index_in_dim(x_rows, 1 - core, 0, keepdims=False)
    far = gather_far(w_qkv)
    rows_own, rows_other, far = lax.optimization_barrier((rows_own, rows_other, far))
    x_own, x_other = rows_own.T, rows_other.T
    w_own = gather_near(far)
    w_other = swap_cores(w_own)
    key_value = dot32(x_own, w_own[:, q_width:]) + dot32(x_other, w_other[:, q_width:])
    key_value = key_value.astype(jnp.bfloat16)
    prior = from_behind(key_value, "seq", 1)
    queries = dot32(x_own, w_own[:, :q_width]) + dot32(x_other, w_other[:, :q_width])
    queries = queries.astype(jnp.bfloat16).reshape(tok_rows, heads, head_dim)
    key_rows = jnp.concatenate([prior[:, :head_dim], key_value[:, :head_dim]], axis=0)
    value_rows = jnp.concatenate([prior[:, head_dim:], key_value[:, head_dim:]], axis=0)
    key_pos = jnp.concatenate([positions - tok_rows, positions])
    grad_query, grad_keys, grad_values, log_total, row_dot = local_pass(
        queries, key_rows, value_rows, out_grad, doc_first, positions, key_pos
    )
    returned = from_behind(
        jnp.concatenate([grad_keys[:tok_rows], grad_values[:tok_rows]], axis=1).astype(
            jnp.bfloat16
        ),
        "seq",
        -1,
    ).astype(jnp.float32)
    far_keys = returned[:, :head_dim]
    far_values = returned[:, head_dim:]
    key_grad = (grad_keys[tok_rows:] + far_keys).astype(jnp.bfloat16)
    value_grad = (grad_values[tok_rows:] + far_values).astype(jnp.bfloat16)
    low_query = grad_query.astype(jnp.bfloat16).reshape(tok_rows, q_width)
    low_kv = jnp.concatenate([key_grad, value_grad], axis=1)
    grad_proj = jnp.concatenate([low_query, low_kv], axis=1)
    received = [
        swap_cores(dot32(rows_other, part).astype(jnp.bfloat16)) for part in (low_query, low_kv)
    ]
    own = lax.optimization_barrier(dot32(rows_own, grad_proj).astype(jnp.bfloat16))
    total = own.astype(jnp.float32) + jnp.concatenate(received, axis=1).astype(jnp.float32)
    weight_grad = scatter_total(total.astype(jnp.bfloat16))
    full_weights = in_order(
        jnp.where(core == 0, w_own, w_other), jnp.where(core == 0, w_other, w_own)
    )
    input_grad = lax.dot_general(
        grad_proj, full_weights, (((1,), (1,)), ((), ())), preferred_element_type=jnp.float32
    )
    input_grad = input_grad.astype(jnp.bfloat16).reshape(1, tok_rows, x_local.shape[1])
    return (input_grad, weight_grad)


def solution(mesh):
    return jax.shard_map(
        body,
        mesh=mesh,
        in_specs=(
            P("dp", "seq", None),
            P("dp", "seq"),
            P(("seq", "dp"), None),
            P("dp", "seq", None),
        ),
        out_specs=(P("dp", "seq", None), P(("seq", "dp"), None)),
        check_vma=False,
    )
```

```python
import jax
import jax.numpy as jnp
from jax import lax
from jax.sharding import PartitionSpec as P

WIN = 256


def from_behind(block, axis, distance):
    devices = range(lax.axis_size(axis))
    route = [(i - distance, i) for i in devices if i - distance in devices]
    return lax.ppermute(block, axis, route)


def masked_scores(queries, key_rows, doc_first, query_pos, key_pos):
    inv_root = queries.shape[2] ** (-0.5)
    scores = (
        jnp.einsum("rhd,kd->hrk", queries, key_rows, preferred_element_type=jnp.float32) * inv_root
    )
    visible = (
        (key_pos[None, :] <= query_pos[:, None])
        & (key_pos[None, :] > query_pos[:, None] - WIN)
        & (key_pos[None, :] >= doc_first[:, None])
    )
    return jnp.where(visible[None, :, :], scores, -jnp.inf)


def backward_terms(queries, key_rows, value_rows, out_grad, attn_probs, prob_low, row_dot):
    inv_root = queries.shape[2] ** (-0.5)
    prob_grad = jnp.einsum("rhd,kd->hrk", out_grad, value_rows, preferred_element_type=jnp.float32)
    score_grad = (attn_probs * (prob_grad - row_dot[:, :, None])).astype(jnp.bfloat16)
    grad_query = (
        jnp.einsum("hrk,kd->rhd", score_grad, key_rows, preferred_element_type=jnp.float32)
        * inv_root
    )
    grad_keys = (
        jnp.einsum("hrk,rhd->kd", score_grad, queries, preferred_element_type=jnp.float32)
        * inv_root
    )
    grad_values = jnp.einsum("hrk,rhd->kd", prob_low, out_grad, preferred_element_type=jnp.float32)
    return (grad_query, grad_keys, grad_values)


def local_pass(queries, key_rows, value_rows, out_grad, doc_first, query_pos, key_pos):
    scores = masked_scores(queries, key_rows, doc_first, query_pos, key_pos)
    row_max = jnp.max(scores, axis=2)
    log_total = row_max + jnp.log(jnp.sum(jnp.exp(scores - row_max[:, :, None]), axis=2))
    attn_probs = jnp.exp(scores - log_total[:, :, None])
    prob_low = attn_probs.astype(jnp.bfloat16)
    context = jnp.einsum("hrk,kd->rhd", prob_low, value_rows, preferred_element_type=jnp.float32)
    row_dot = jnp.sum(out_grad.astype(jnp.float32) * context, axis=2).T
    grad_query, grad_keys, grad_values = backward_terms(
        queries, key_rows, value_rows, out_grad, attn_probs, prob_low, row_dot
    )
    return (grad_query, grad_keys, grad_values, log_total, row_dot)


AXES = ("seq", "dp")


def spot(y, z, core, x):
    return ((y % 8 * 8 + z % 8) * 2 + core) * 4 + x % 4


def far_groups():
    return [
        [spot(2 * y + a, 2 * z + b, core, 2 * x + d) for y in range(4) for z in range(4) for x in range(2)]
        for a in range(2)
        for b in range(2)
        for core in range(2)
        for d in range(2)
    ]


def near_groups():
    groups = []
    for core in range(2):
        for y in range(4):
            for z in range(4):
                for x in range(2):
                    low = [(k, k) if core == 0 else (k, 2 - k) for k in range(2)]
                    groups.append(
                        [
                            spot(2 * y + a[1], 2 * z + b[1], core, 2 * x + d[1])
                            for a in low
                            for b in low
                            for d in low
                        ]
                    )
    return groups


def exchange(blocks, groups):
    return lax.all_to_all(blocks, AXES, 0, 0, axis_index_groups=groups)


def swap_cores(block):
    count = lax.axis_size("seq")
    return lax.ppermute(block, "seq", [(i, i ^ 1) for i in range(count)])


def gather_far(w_block):
    far = exchange(jnp.broadcast_to(w_block, (32,) + w_block.shape), far_groups())
    return far.reshape(32 * w_block.shape[0], w_block.shape[1])


def gather_near(far):
    own = exchange(jnp.broadcast_to(far, (8,) + far.shape), near_groups())
    return own.reshape(8 * far.shape[0], far.shape[1])


def by_holder(x_local):
    tokens, width = x_local.shape
    rows = width // 512
    split = x_local.T.reshape(4, 2, 4, 2, 2, 2, 2, rows, tokens)
    return split.transpose(4, 1, 3, 6, 0, 2, 5, 7, 8).reshape(2, 256 * rows, tokens)


def in_order(own, other, core):
    rows, width = own.shape[0] // 256, own.shape[1]
    full = jnp.zeros((4, 2, 4, 2, 2, 2, 2, rows, width), own.dtype)
    for part, place in ((own, core), (other, 1 - core)):
        part = part.reshape(2, 2, 2, 4, 4, 2, rows, width).transpose(3, 0, 4, 1, 5, 2, 6, 7)
        full = lax.dynamic_update_slice_in_dim(full, part[:, :, :, :, None], place, 4)
    return full.reshape(512 * rows, width)


def scatter_near(total):
    rows, width = total.shape[0] // 8, total.shape[1]
    return exchange(total.reshape(8, rows, width), near_groups())


def scatter_far(blocks):
    total = jnp.sum(blocks.astype(jnp.float32), axis=0).astype(jnp.bfloat16)
    total = total.reshape(32, total.shape[0] // 32, total.shape[1])
    return jnp.sum(exchange(total, far_groups()).astype(jnp.float32), axis=0)


def dot32(a, b):
    return jnp.dot(a, b, preferred_element_type=jnp.float32)


def body(layer_inputs, doc_start, w_qkv, d_context):
    x_local = layer_inputs[0]
    tok_rows = x_local.shape[0]
    q_width = d_context.shape[2]
    head_dim = (w_qkv.shape[1] - q_width) // 2
    heads = q_width // head_dim
    out_grad = d_context[0].reshape(tok_rows, heads, head_dim)
    doc_first = doc_start[0]
    positions = lax.axis_index("seq") * tok_rows + jnp.arange(tok_rows, dtype=jnp.int32)
    core = lax.axis_index("seq") & 1
    x_rows = by_holder(x_local)
    rows_own = lax.dynamic_index_in_dim(x_rows, core, 0, keepdims=False)
    rows_other = lax.dynamic_index_in_dim(x_rows, 1 - core, 0, keepdims=False)
    far = gather_far(w_qkv)
    rows_own, rows_other, far = lax.optimization_barrier((rows_own, rows_other, far))
    x_own, x_other = rows_own.T, rows_other.T
    w_own = gather_near(far)
    w_other = swap_cores(w_own)
    projected = dot32(x_own, w_own) + dot32(x_other, w_other)
    projected = projected.astype(jnp.bfloat16)
    queries = projected[:, :q_width].reshape(tok_rows, heads, head_dim)
    key_value = projected[:, q_width:]
    prior = from_behind(key_value, "seq", 1)
    key_rows = jnp.concatenate([prior[:, :head_dim], key_value[:, :head_dim]], axis=0)
    value_rows = jnp.concatenate([prior[:, head_dim:], key_value[:, head_dim:]], axis=0)
    key_pos = jnp.concatenate([positions - tok_rows, positions])
    grad_query, grad_keys, grad_values, log_total, row_dot = local_pass(
        queries, key_rows, value_rows, out_grad, doc_first, positions, key_pos
    )
    returned = from_behind(
        jnp.concatenate([grad_keys[:tok_rows], grad_values[:tok_rows]], axis=1).astype(
            jnp.bfloat16
        ),
        "seq",
        -1,
    ).astype(jnp.float32)
    far_keys = returned[:, :head_dim]
    far_values = returned[:, head_dim:]
    key_grad = (grad_keys[tok_rows:] + far_keys).astype(jnp.bfloat16)
    value_grad = (grad_values[tok_rows:] + far_values).astype(jnp.bfloat16)
    low_query = grad_query.astype(jnp.bfloat16).reshape(tok_rows, q_width)
    low_kv = jnp.concatenate([key_grad, value_grad], axis=1)
    grad_proj = jnp.concatenate([low_query, low_kv], axis=1)
    received = [
        swap_cores(dot32(rows_other, part).astype(jnp.bfloat16)) for part in (low_query, low_kv)
    ]
    own = lax.optimization_barrier(dot32(rows_own, grad_proj).astype(jnp.bfloat16))
    total = own.astype(jnp.float32) + jnp.concatenate(received, axis=1).astype(jnp.float32)
    blocks = scatter_near(total.astype(jnp.bfloat16))
    blocks, w_own, w_other = lax.optimization_barrier((blocks, w_own, w_other))
    weight_grad = scatter_far(blocks)
    full_weights = in_order(w_own, w_other, core)
    input_grad = lax.dot_general(
        grad_proj, full_weights, (((1,), (1,)), ((), ())), preferred_element_type=jnp.float32
    )
    input_grad = input_grad.astype(jnp.bfloat16).reshape(1, tok_rows, x_local.shape[1])
    return (input_grad, weight_grad)


def solution(mesh):
    return jax.shard_map(
        body,
        mesh=mesh,
        in_specs=(
            P("dp", "seq", None),
            P("dp", "seq"),
            P(("seq", "dp"), None),
            P("dp", "seq", None),
        ),
        out_specs=(P("dp", "seq", None), P(("seq", "dp"), None)),
        check_vma=False,
    )
```

```python
import jax
import jax.numpy as jnp
from jax import lax
from jax.sharding import PartitionSpec as P

WIN = 256


def from_behind(block, axis, distance):
    devices = range(lax.axis_size(axis))
    route = [(i - distance, i) for i in devices if i - distance in devices]
    return lax.ppermute(block, axis, route)


def masked_scores(queries, key_rows, doc_first, query_pos, key_pos):
    inv_root = queries.shape[2] ** (-0.5)
    scores = (
        jnp.einsum("rhd,kd->hrk", queries, key_rows, preferred_element_type=jnp.float32) * inv_root
    )
    visible = (
        (key_pos[None, :] <= query_pos[:, None])
        & (key_pos[None, :] > query_pos[:, None] - WIN)
        & (key_pos[None, :] >= doc_first[:, None])
    )
    return jnp.where(visible[None, :, :], scores, -jnp.inf)


def backward_terms(queries, key_rows, value_rows, out_grad, attn_probs, prob_low, row_dot):
    inv_root = queries.shape[2] ** (-0.5)
    prob_grad = jnp.einsum("rhd,kd->hrk", out_grad, value_rows, preferred_element_type=jnp.float32)
    score_grad = (attn_probs * (prob_grad - row_dot[:, :, None])).astype(jnp.bfloat16)
    grad_query = (
        jnp.einsum("hrk,kd->rhd", score_grad, key_rows, preferred_element_type=jnp.float32)
        * inv_root
    )
    grad_keys = (
        jnp.einsum("hrk,rhd->kd", score_grad, queries, preferred_element_type=jnp.float32)
        * inv_root
    )
    grad_values = jnp.einsum("hrk,rhd->kd", prob_low, out_grad, preferred_element_type=jnp.float32)
    return (grad_query, grad_keys, grad_values)


def local_pass(queries, key_rows, value_rows, out_grad, doc_first, query_pos, key_pos):
    scores = masked_scores(queries, key_rows, doc_first, query_pos, key_pos)
    row_max = jnp.max(scores, axis=2)
    log_total = row_max + jnp.log(jnp.sum(jnp.exp(scores - row_max[:, :, None]), axis=2))
    attn_probs = jnp.exp(scores - log_total[:, :, None])
    prob_low = attn_probs.astype(jnp.bfloat16)
    context = jnp.einsum("hrk,kd->rhd", prob_low, value_rows, preferred_element_type=jnp.float32)
    row_dot = jnp.sum(out_grad.astype(jnp.float32) * context, axis=2).T
    grad_query, grad_keys, grad_values = backward_terms(
        queries, key_rows, value_rows, out_grad, attn_probs, prob_low, row_dot
    )
    return (grad_query, grad_keys, grad_values, log_total, row_dot)


AXES = ("seq", "dp")


def spot(y, z, core, x):
    return ((y % 8 * 8 + z % 8) * 2 + core) * 4 + x % 4


def far_groups():
    return [
        [spot(2 * y + a, 2 * z + b, core, 2 * x + d) for y in range(4) for z in range(4) for x in range(2)]
        for a in range(2)
        for b in range(2)
        for core in range(2)
        for d in range(2)
    ]


def near_groups():
    groups = []
    for core in range(2):
        for y in range(4):
            for z in range(4):
                for x in range(2):
                    low = [(k, k) if core == 0 else (k, 2 - k) for k in range(2)]
                    groups.append(
                        [
                            spot(2 * y + a[1], 2 * z + b[1], core, 2 * x + d[1])
                            for a in low
                            for b in low
                            for d in low
                        ]
                    )
    return groups


def exchange(blocks, groups):
    return lax.all_to_all(blocks, AXES, 0, 0, axis_index_groups=groups)


def swap_cores(block):
    count = lax.axis_size("seq")
    return lax.ppermute(block, "seq", [(i, i ^ 1) for i in range(count)])


def gather_far(w_block):
    far = exchange(jnp.broadcast_to(w_block, (32,) + w_block.shape), far_groups())
    return far.reshape(32 * w_block.shape[0], w_block.shape[1])


def gather_near(far):
    own = exchange(jnp.broadcast_to(far, (8,) + far.shape), near_groups())
    return own.reshape(8 * far.shape[0], far.shape[1])


def by_holder(x_local):
    tokens, width = x_local.shape
    rows = width // 512
    split = x_local.T.reshape(4, 2, 4, 2, 2, 2, 2, rows, tokens)
    return split.transpose(4, 1, 3, 6, 0, 2, 5, 7, 8).reshape(2, 256 * rows, tokens)


def in_order(own, other, core):
    rows, width = own.shape[0] // 256, own.shape[1]
    full = jnp.zeros((4, 2, 4, 2, 2, 2, 2, rows, width), own.dtype)
    for part, place in ((own, core), (other, 1 - core)):
        part = part.reshape(2, 2, 2, 4, 4, 2, rows, width).transpose(3, 0, 4, 1, 5, 2, 6, 7)
        full = lax.dynamic_update_slice_in_dim(full, part[:, :, :, :, None], place, 4)
    return full.reshape(512 * rows, width)


def scatter_near(total):
    rows, width = total.shape[0] // 8, total.shape[1]
    return exchange(total.reshape(8, rows, width), near_groups())


def scatter_far(blocks):
    total = jnp.sum(blocks.astype(jnp.float32), axis=0).astype(jnp.bfloat16)
    total = total.reshape(32, total.shape[0] // 32, total.shape[1])
    return jnp.sum(exchange(total, far_groups()).astype(jnp.float32), axis=0)


def dot32(a, b):
    return jnp.dot(a, b, preferred_element_type=jnp.float32)


def body(layer_inputs, doc_start, w_qkv, d_context):
    x_local = layer_inputs[0]
    tok_rows = x_local.shape[0]
    q_width = d_context.shape[2]
    head_dim = (w_qkv.shape[1] - q_width) // 2
    heads = q_width // head_dim
    out_grad = d_context[0].reshape(tok_rows, heads, head_dim)
    doc_first = doc_start[0]
    positions = lax.axis_index("seq") * tok_rows + jnp.arange(tok_rows, dtype=jnp.int32)
    core = lax.axis_index("seq") & 1
    x_rows = by_holder(x_local)
    rows_own = lax.dynamic_index_in_dim(x_rows, core, 0, keepdims=False)
    rows_other = lax.dynamic_index_in_dim(x_rows, 1 - core, 0, keepdims=False)
    far = gather_far(w_qkv)
    rows_own, rows_other, far = lax.optimization_barrier((rows_own, rows_other, far))
    x_own, x_other = rows_own.T, rows_other.T
    w_own = gather_near(far)
    w_other = swap_cores(w_own)
    projected = dot32(x_own, w_own) + dot32(x_other, w_other)
    projected = projected.astype(jnp.bfloat16)
    queries = projected[:, :q_width].reshape(tok_rows, heads, head_dim)
    key_value = projected[:, q_width:]
    prior, full_weights = lax.optimization_barrier(
        (from_behind(key_value, "seq", 1), in_order(w_own, w_other, core))
    )
    key_rows = jnp.concatenate([prior[:, :head_dim], key_value[:, :head_dim]], axis=0)
    value_rows = jnp.concatenate([prior[:, head_dim:], key_value[:, head_dim:]], axis=0)
    key_pos = jnp.concatenate([positions - tok_rows, positions])
    grad_query, grad_keys, grad_values, log_total, row_dot = local_pass(
        queries, key_rows, value_rows, out_grad, doc_first, positions, key_pos
    )
    returned = from_behind(
        jnp.concatenate([grad_keys[:tok_rows], grad_values[:tok_rows]], axis=1).astype(
            jnp.bfloat16
        ),
        "seq",
        -1,
    ).astype(jnp.float32)
    far_keys = returned[:, :head_dim]
    far_values = returned[:, head_dim:]
    key_grad = (grad_keys[tok_rows:] + far_keys).astype(jnp.bfloat16)
    value_grad = (grad_values[tok_rows:] + far_values).astype(jnp.bfloat16)
    low_query = grad_query.astype(jnp.bfloat16).reshape(tok_rows, q_width)
    low_kv = jnp.concatenate([key_grad, value_grad], axis=1)
    grad_proj = jnp.concatenate([low_query, low_kv], axis=1)
    received = [
        swap_cores(dot32(rows_other, part).astype(jnp.bfloat16)) for part in (low_query, low_kv)
    ]
    own = lax.optimization_barrier(dot32(rows_own, grad_proj).astype(jnp.bfloat16))
    total = own.astype(jnp.float32) + jnp.concatenate(received, axis=1).astype(jnp.float32)
    blocks = scatter_near(total.astype(jnp.bfloat16))
    blocks, full_weights = lax.optimization_barrier((blocks, full_weights))
    weight_grad = scatter_far(blocks)
    input_grad = lax.dot_general(
        grad_proj, full_weights, (((1,), (1,)), ((), ())), preferred_element_type=jnp.float32
    )
    input_grad = input_grad.astype(jnp.bfloat16).reshape(1, tok_rows, x_local.shape[1])
    return (input_grad, weight_grad)


def solution(mesh):
    return jax.shard_map(
        body,
        mesh=mesh,
        in_specs=(
            P("dp", "seq", None),
            P("dp", "seq"),
            P(("seq", "dp"), None),
            P("dp", "seq", None),
        ),
        out_specs=(P("dp", "seq", None), P(("seq", "dp"), None)),
        check_vma=False,
    )
```

```python
import jax
import jax.numpy as jnp
from jax import lax
from jax.experimental import pallas as pl
from jax.experimental.pallas import tpu as pltpu
from jax.sharding import PartitionSpec as P

WIN = 256


def from_behind(block, axis, distance):
    devices = range(lax.axis_size(axis))
    route = [(i - distance, i) for i in devices if i - distance in devices]
    return lax.ppermute(block, axis, route)


def masked_scores(queries, key_rows, doc_first, query_pos, key_pos):
    inv_root = queries.shape[2] ** (-0.5)
    scores = (
        jnp.einsum("rhd,kd->hrk", queries, key_rows, preferred_element_type=jnp.float32) * inv_root
    )
    visible = (
        (key_pos[None, :] <= query_pos[:, None])
        & (key_pos[None, :] > query_pos[:, None] - WIN)
        & (key_pos[None, :] >= doc_first[:, None])
    )
    return jnp.where(visible[None, :, :], scores, -jnp.inf)


def backward_terms(queries, key_rows, value_rows, out_grad, attn_probs, prob_low, row_dot):
    inv_root = queries.shape[2] ** (-0.5)
    prob_grad = jnp.einsum("rhd,kd->hrk", out_grad, value_rows, preferred_element_type=jnp.float32)
    score_grad = (attn_probs * (prob_grad - row_dot[:, :, None])).astype(jnp.bfloat16)
    grad_query = (
        jnp.einsum("hrk,kd->rhd", score_grad, key_rows, preferred_element_type=jnp.float32)
        * inv_root
    )
    grad_keys = (
        jnp.einsum("hrk,rhd->kd", score_grad, queries, preferred_element_type=jnp.float32)
        * inv_root
    )
    grad_values = jnp.einsum("hrk,rhd->kd", prob_low, out_grad, preferred_element_type=jnp.float32)
    return (grad_query, grad_keys, grad_values)


def local_pass(queries, key_rows, value_rows, out_grad, doc_first, query_pos, key_pos):
    scores = masked_scores(queries, key_rows, doc_first, query_pos, key_pos)
    row_max = jnp.max(scores, axis=2)
    log_total = row_max + jnp.log(jnp.sum(jnp.exp(scores - row_max[:, :, None]), axis=2))
    attn_probs = jnp.exp(scores - log_total[:, :, None])
    prob_low = attn_probs.astype(jnp.bfloat16)
    context = jnp.einsum("hrk,kd->rhd", prob_low, value_rows, preferred_element_type=jnp.float32)
    row_dot = jnp.sum(out_grad.astype(jnp.float32) * context, axis=2).T
    grad_query, grad_keys, grad_values = backward_terms(
        queries, key_rows, value_rows, out_grad, attn_probs, prob_low, row_dot
    )
    return (grad_query, grad_keys, grad_values, log_total, row_dot)


AXES = ("seq", "dp")


def spot(y, z, core, x):
    return ((y % 8 * 8 + z % 8) * 2 + core) * 4 + x % 4


def far_groups():
    return [
        [spot(2 * y + a, 2 * z + b, core, 2 * x + d) for y in range(4) for z in range(4) for x in range(2)]
        for a in range(2)
        for b in range(2)
        for core in range(2)
        for d in range(2)
    ]


def near_groups():
    groups = []
    for core in range(2):
        for y in range(4):
            for z in range(4):
                for x in range(2):
                    low = [(k, k) if core == 0 else (k, 2 - k) for k in range(2)]
                    groups.append(
                        [
                            spot(2 * y + a[1], 2 * z + b[1], core, 2 * x + d[1])
                            for a in low
                            for b in low
                            for d in low
                        ]
                    )
    return groups


def exchange(blocks, groups):
    return lax.all_to_all(blocks, AXES, 0, 0, axis_index_groups=groups)


def swap_cores(block):
    count = lax.axis_size("seq")
    return lax.ppermute(block, "seq", [(i, i ^ 1) for i in range(count)])


def gather_far(w_block):
    far = exchange(jnp.broadcast_to(w_block, (32,) + w_block.shape), far_groups())
    return far.reshape(32 * w_block.shape[0], w_block.shape[1])


def gather_near(far):
    own = exchange(jnp.broadcast_to(far, (8,) + far.shape), near_groups())
    return own.reshape(8 * far.shape[0], far.shape[1])


def by_holder(x_local):
    tokens, width = x_local.shape
    rows = width // 512
    split = x_local.T.reshape(4, 2, 4, 2, 2, 2, 2, rows, tokens)
    return split.transpose(4, 1, 3, 6, 0, 2, 5, 7, 8).reshape(2, 256 * rows, tokens)


def in_order(own, other, core):
    rows, width = own.shape[0] // 256, own.shape[1]
    full = jnp.zeros((4, 2, 4, 2, 2, 2, 2, rows, width), own.dtype)
    for part, place in ((own, core), (other, 1 - core)):
        part = part.reshape(2, 2, 2, 4, 4, 2, rows, width).transpose(3, 0, 4, 1, 5, 2, 6, 7)
        full = lax.dynamic_update_slice_in_dim(full, part[:, :, :, :, None], place, 4)
    return full.reshape(512 * rows, width)


def scatter_near(total):
    rows, width = total.shape[0] // 8, total.shape[1]
    return exchange(total.reshape(8, rows, width), near_groups())


def scatter_far(blocks):
    total = jnp.sum(blocks.astype(jnp.float32), axis=0).astype(jnp.bfloat16)
    total = total.reshape(32, total.shape[0] // 32, total.shape[1])
    return jnp.sum(exchange(total, far_groups()).astype(jnp.float32), axis=0)


def dot32(a, b):
    return jnp.dot(a, b, preferred_element_type=jnp.float32)


def add_product_kernel(start_ref, rows_ref, weights_ref, out_ref, sum_ref):
    step = pl.program_id(0)

    @pl.when(step == 0)
    def _():
        sum_ref[...] = start_ref[...]

    sum_ref[...] += lax.dot_general(
        rows_ref[...],
        weights_ref[...],
        (((0,), (0,)), ((), ())),
        preferred_element_type=jnp.float32,
    )

    @pl.when(step == pl.num_programs(0) - 1)
    def _():
        out_ref[...] = sum_ref[...].astype(out_ref.dtype)


def add_product(start, rows, weights):
    depth, tokens = rows.shape
    width = weights.shape[1]
    chunk = depth // 4
    whole = pl.BlockSpec((tokens, width), lambda i: (0, 0))
    return pl.pallas_call(
        add_product_kernel,
        out_shape=jax.ShapeDtypeStruct((tokens, width), jnp.bfloat16),
        grid=(depth // chunk,),
        in_specs=[
            whole,
            pl.BlockSpec((chunk, tokens), lambda i: (i, 0)),
            pl.BlockSpec((chunk, width), lambda i: (i, 0)),
        ],
        out_specs=whole,
        scratch_shapes=[pltpu.VMEM((tokens, width), jnp.float32)],
        cost_estimate=pl.CostEstimate(
            flops=2 * depth * tokens * width,
            bytes_accessed=2 * depth * (tokens + width) + 6 * tokens * width,
            transcendentals=0,
        ),
    )(start, rows, weights)


def body(layer_inputs, doc_start, w_qkv, d_context):
    x_local = layer_inputs[0]
    tok_rows = x_local.shape[0]
    q_width = d_context.shape[2]
    head_dim = (w_qkv.shape[1] - q_width) // 2
    heads = q_width // head_dim
    out_grad = d_context[0].reshape(tok_rows, heads, head_dim)
    doc_first = doc_start[0]
    positions = lax.axis_index("seq") * tok_rows + jnp.arange(tok_rows, dtype=jnp.int32)
    core = lax.axis_index("seq") & 1
    x_rows = by_holder(x_local)
    rows_own = lax.dynamic_index_in_dim(x_rows, core, 0, keepdims=False)
    rows_other = lax.dynamic_index_in_dim(x_rows, 1 - core, 0, keepdims=False)
    far = gather_far(w_qkv)
    rows_own, rows_other, far = lax.optimization_barrier((rows_own, rows_other, far))
    w_own = gather_near(far)
    w_other = swap_cores(w_own)
    projected = add_product(dot32(rows_own.T, w_own), rows_other, w_other)
    queries = projected[:, :q_width].reshape(tok_rows, heads, head_dim)
    key_value = projected[:, q_width:]
    prior = from_behind(key_value, "seq", 1)
    key_rows = jnp.concatenate([prior[:, :head_dim], key_value[:, :head_dim]], axis=0)
    value_rows = jnp.concatenate([prior[:, head_dim:], key_value[:, head_dim:]], axis=0)
    key_pos = jnp.concatenate([positions - tok_rows, positions])
    grad_query, grad_keys, grad_values, log_total, row_dot = local_pass(
        queries, key_rows, value_rows, out_grad, doc_first, positions, key_pos
    )
    returned = from_behind(
        jnp.concatenate([grad_keys[:tok_rows], grad_values[:tok_rows]], axis=1).astype(
            jnp.bfloat16
        ),
        "seq",
        -1,
    ).astype(jnp.float32)
    far_keys = returned[:, :head_dim]
    far_values = returned[:, head_dim:]
    key_grad = (grad_keys[tok_rows:] + far_keys).astype(jnp.bfloat16)
    value_grad = (grad_values[tok_rows:] + far_values).astype(jnp.bfloat16)
    low_query = grad_query.astype(jnp.bfloat16).reshape(tok_rows, q_width)
    low_kv = jnp.concatenate([key_grad, value_grad], axis=1)
    grad_proj = jnp.concatenate([low_query, low_kv], axis=1)
    received = [
        swap_cores(dot32(rows_other, part).astype(jnp.bfloat16)) for part in (low_query, low_kv)
    ]
    own = lax.optimization_barrier(dot32(rows_own, grad_proj).astype(jnp.bfloat16))
    total = own.astype(jnp.float32) + jnp.concatenate(received, axis=1).astype(jnp.float32)
    blocks = scatter_near(total.astype(jnp.bfloat16))
    blocks, w_own, w_other = lax.optimization_barrier((blocks, w_own, w_other))
    weight_grad = scatter_far(blocks)
    full_weights = in_order(w_own, w_other, core)
    input_grad = lax.dot_general(
        grad_proj, full_weights, (((1,), (1,)), ((), ())), preferred_element_type=jnp.float32
    )
    input_grad = input_grad.astype(jnp.bfloat16).reshape(1, tok_rows, x_local.shape[1])
    return (input_grad, weight_grad)


def solution(mesh):
    return jax.shard_map(
        body,
        mesh=mesh,
        in_specs=(
            P("dp", "seq", None),
            P("dp", "seq"),
            P(("seq", "dp"), None),
            P("dp", "seq", None),
        ),
        out_specs=(P("dp", "seq", None), P(("seq", "dp"), None)),
        check_vma=False,
    )
```

```python
import jax
import jax.numpy as jnp
from jax import lax
from jax.sharding import PartitionSpec as P

WIN = 256


def from_behind(block, axis, distance):
    devices = range(lax.axis_size(axis))
    route = [(i - distance, i) for i in devices if i - distance in devices]
    return lax.ppermute(block, axis, route)


def masked_scores(queries, key_rows, doc_first, query_pos, key_pos):
    inv_root = queries.shape[2] ** (-0.5)
    scores = (
        jnp.einsum("rhd,kd->hrk", queries, key_rows, preferred_element_type=jnp.float32) * inv_root
    )
    visible = (
        (key_pos[None, :] <= query_pos[:, None])
        & (key_pos[None, :] > query_pos[:, None] - WIN)
        & (key_pos[None, :] >= doc_first[:, None])
    )
    return jnp.where(visible[None, :, :], scores, -jnp.inf)


def backward_terms(queries, key_rows, value_rows, out_grad, attn_probs, prob_low, row_dot):
    inv_root = queries.shape[2] ** (-0.5)
    prob_grad = jnp.einsum("rhd,kd->hrk", out_grad, value_rows, preferred_element_type=jnp.float32)
    score_grad = (attn_probs * (prob_grad - row_dot[:, :, None])).astype(jnp.bfloat16)
    grad_query = (
        jnp.einsum("hrk,kd->rhd", score_grad, key_rows, preferred_element_type=jnp.float32)
        * inv_root
    )
    grad_keys = (
        jnp.einsum("hrk,rhd->kd", score_grad, queries, preferred_element_type=jnp.float32)
        * inv_root
    )
    grad_values = jnp.einsum("hrk,rhd->kd", prob_low, out_grad, preferred_element_type=jnp.float32)
    return (grad_query, grad_keys, grad_values)


def local_pass(queries, key_rows, value_rows, out_grad, doc_first, query_pos, key_pos):
    scores = masked_scores(queries, key_rows, doc_first, query_pos, key_pos)
    row_max = jnp.max(scores, axis=2)
    log_total = row_max + jnp.log(jnp.sum(jnp.exp(scores - row_max[:, :, None]), axis=2))
    attn_probs = jnp.exp(scores - log_total[:, :, None])
    prob_low = attn_probs.astype(jnp.bfloat16)
    context = jnp.einsum("hrk,kd->rhd", prob_low, value_rows, preferred_element_type=jnp.float32)
    row_dot = jnp.sum(out_grad.astype(jnp.float32) * context, axis=2).T
    grad_query, grad_keys, grad_values = backward_terms(
        queries, key_rows, value_rows, out_grad, attn_probs, prob_low, row_dot
    )
    return (grad_query, grad_keys, grad_values, log_total, row_dot)


AXES = ("seq", "dp")


def spot(y, z, core, x):
    return ((y % 8 * 8 + z % 8) * 2 + core) * 4 + x % 4


def far_groups():
    return [
        [spot(2 * y + a, 2 * z + b, core, 2 * x + d) for y in range(4) for z in range(4) for x in range(2)]
        for a in range(2)
        for b in range(2)
        for core in range(2)
        for d in range(2)
    ]


def near_groups():
    groups = []
    for core in range(2):
        pair = [[(k, 2 - k if odd else k) for k in range(2)] for odd in (core, 1 - core, core)]
        for y in range(4):
            for z in range(4):
                for x in range(2):
                    groups.append(
                        [
                            spot(2 * y + a[1], 2 * z + b[1], core, 2 * x + d[1])
                            for a in pair[0]
                            for b in pair[1]
                            for d in pair[2]
                        ]
                    )
    return groups


def exchange(blocks, groups):
    return lax.all_to_all(blocks, AXES, 0, 0, axis_index_groups=groups)


def swap_cores(block):
    count = lax.axis_size("seq")
    return lax.ppermute(block, "seq", [(i, i ^ 1) for i in range(count)])


def gather_far(w_block):
    far = exchange(jnp.broadcast_to(w_block, (32,) + w_block.shape), far_groups())
    return far.reshape(32 * w_block.shape[0], w_block.shape[1])


def gather_near(far):
    own = exchange(jnp.broadcast_to(far, (8,) + far.shape), near_groups())
    return own.reshape(8 * far.shape[0], far.shape[1])


def by_holder(x_local):
    tokens, width = x_local.shape
    rows = width // 512
    split = x_local.T.reshape(4, 2, 4, 2, 2, 2, 2, rows, tokens)
    return split.transpose(4, 1, 3, 6, 0, 2, 5, 7, 8).reshape(2, 256 * rows, tokens)


def in_order(own, other, core):
    rows, width = own.shape[0] // 256, own.shape[1]
    full = jnp.zeros((4, 2, 4, 2, 2, 2, 2, rows, width), own.dtype)
    for part, place in ((own, core), (other, 1 - core)):
        part = part.reshape(2, 2, 2, 4, 4, 2, rows, width).transpose(3, 0, 4, 1, 5, 2, 6, 7)
        full = lax.dynamic_update_slice_in_dim(full, part[:, :, :, :, None], place, 4)
    return full.reshape(512 * rows, width)


def scatter_near(total):
    rows, width = total.shape[0] // 8, total.shape[1]
    return exchange(total.reshape(8, rows, width), near_groups())


def scatter_far(blocks):
    total = jnp.sum(blocks.astype(jnp.float32), axis=0).astype(jnp.bfloat16)
    total = total.reshape(32, total.shape[0] // 32, total.shape[1])
    return jnp.sum(exchange(total, far_groups()).astype(jnp.float32), axis=0)


def dot32(a, b):
    return jnp.dot(a, b, preferred_element_type=jnp.float32)


def body(layer_inputs, doc_start, w_qkv, d_context):
    x_local = layer_inputs[0]
    tok_rows = x_local.shape[0]
    q_width = d_context.shape[2]
    head_dim = (w_qkv.shape[1] - q_width) // 2
    heads = q_width // head_dim
    out_grad = d_context[0].reshape(tok_rows, heads, head_dim)
    doc_first = doc_start[0]
    positions = lax.axis_index("seq") * tok_rows + jnp.arange(tok_rows, dtype=jnp.int32)
    core = lax.axis_index("seq") & 1
    x_rows = by_holder(x_local)
    rows_own = lax.dynamic_index_in_dim(x_rows, core, 0, keepdims=False)
    rows_other = lax.dynamic_index_in_dim(x_rows, 1 - core, 0, keepdims=False)
    far = gather_far(w_qkv)
    rows_own, rows_other, far = lax.optimization_barrier((rows_own, rows_other, far))
    x_own, x_other = rows_own.T, rows_other.T
    w_own = gather_near(far)
    w_other = swap_cores(w_own)
    projected = dot32(x_own, w_own) + dot32(x_other, w_other)
    projected = projected.astype(jnp.bfloat16)
    queries = projected[:, :q_width].reshape(tok_rows, heads, head_dim)
    key_value = projected[:, q_width:]
    prior = from_behind(key_value, "seq", 1)
    key_rows = jnp.concatenate([prior[:, :head_dim], key_value[:, :head_dim]], axis=0)
    value_rows = jnp.concatenate([prior[:, head_dim:], key_value[:, head_dim:]], axis=0)
    key_pos = jnp.concatenate([positions - tok_rows, positions])
    grad_query, grad_keys, grad_values, log_total, row_dot = local_pass(
        queries, key_rows, value_rows, out_grad, doc_first, positions, key_pos
    )
    returned = from_behind(
        jnp.concatenate([grad_keys[:tok_rows], grad_values[:tok_rows]], axis=1).astype(
            jnp.bfloat16
        ),
        "seq",
        -1,
    ).astype(jnp.float32)
    far_keys = returned[:, :head_dim]
    far_values = returned[:, head_dim:]
    key_grad = (grad_keys[tok_rows:] + far_keys).astype(jnp.bfloat16)
    value_grad = (grad_values[tok_rows:] + far_values).astype(jnp.bfloat16)
    low_query = grad_query.astype(jnp.bfloat16).reshape(tok_rows, q_width)
    low_kv = jnp.concatenate([key_grad, value_grad], axis=1)
    grad_proj = jnp.concatenate([low_query, low_kv], axis=1)
    received = [
        swap_cores(dot32(rows_other, part).astype(jnp.bfloat16)) for part in (low_query, low_kv)
    ]
    own = lax.optimization_barrier(dot32(rows_own, grad_proj).astype(jnp.bfloat16))
    total = own.astype(jnp.float32) + jnp.concatenate(received, axis=1).astype(jnp.float32)
    blocks = scatter_near(total.astype(jnp.bfloat16))
    blocks, w_own, w_other = lax.optimization_barrier((blocks, w_own, w_other))
    weight_grad = scatter_far(blocks)
    full_weights = in_order(w_own, w_other, core)
    input_grad = lax.dot_general(
        grad_proj, full_weights, (((1,), (1,)), ((), ())), preferred_element_type=jnp.float32
    )
    input_grad = input_grad.astype(jnp.bfloat16).reshape(1, tok_rows, x_local.shape[1])
    return (input_grad, weight_grad)


def solution(mesh):
    return jax.shard_map(
        body,
        mesh=mesh,
        in_specs=(
            P("dp", "seq", None),
            P("dp", "seq"),
            P(("seq", "dp"), None),
            P("dp", "seq", None),
        ),
        out_specs=(P("dp", "seq", None), P(("seq", "dp"), None)),
        check_vma=False,
    )
```

```python
import jax
import jax.numpy as jnp
from jax import lax
from jax.sharding import PartitionSpec as P

WIN = 256


def from_behind(block, axis, distance):
    devices = range(lax.axis_size(axis))
    route = [(i - distance, i) for i in devices if i - distance in devices]
    return lax.ppermute(block, axis, route)


def masked_scores(queries, key_rows, doc_first, query_pos, key_pos):
    inv_root = queries.shape[2] ** (-0.5)
    scores = (
        jnp.einsum("rhd,kd->hrk", queries, key_rows, preferred_element_type=jnp.float32) * inv_root
    )
    visible = (
        (key_pos[None, :] <= query_pos[:, None])
        & (key_pos[None, :] > query_pos[:, None] - WIN)
        & (key_pos[None, :] >= doc_first[:, None])
    )
    return jnp.where(visible[None, :, :], scores, -jnp.inf)


def backward_terms(queries, key_rows, value_rows, out_grad, attn_probs, prob_low, row_dot):
    inv_root = queries.shape[2] ** (-0.5)
    prob_grad = jnp.einsum("rhd,kd->hrk", out_grad, value_rows, preferred_element_type=jnp.float32)
    score_grad = (attn_probs * (prob_grad - row_dot[:, :, None])).astype(jnp.bfloat16)
    grad_query = (
        jnp.einsum("hrk,kd->rhd", score_grad, key_rows, preferred_element_type=jnp.float32)
        * inv_root
    )
    grad_keys = (
        jnp.einsum("hrk,rhd->kd", score_grad, queries, preferred_element_type=jnp.float32)
        * inv_root
    )
    grad_values = jnp.einsum("hrk,rhd->kd", prob_low, out_grad, preferred_element_type=jnp.float32)
    return (grad_query, grad_keys, grad_values)


def local_pass(queries, key_rows, value_rows, out_grad, doc_first, query_pos, key_pos):
    scores = masked_scores(queries, key_rows, doc_first, query_pos, key_pos)
    row_max = jnp.max(scores, axis=2)
    log_total = row_max + jnp.log(jnp.sum(jnp.exp(scores - row_max[:, :, None]), axis=2))
    attn_probs = jnp.exp(scores - log_total[:, :, None])
    prob_low = attn_probs.astype(jnp.bfloat16)
    context = jnp.einsum("hrk,kd->rhd", prob_low, value_rows, preferred_element_type=jnp.float32)
    row_dot = jnp.sum(out_grad.astype(jnp.float32) * context, axis=2).T
    grad_query, grad_keys, grad_values = backward_terms(
        queries, key_rows, value_rows, out_grad, attn_probs, prob_low, row_dot
    )
    return (grad_query, grad_keys, grad_values, log_total, row_dot)


AXES = ("seq", "dp")


def spot(y, z, core, x):
    return ((y % 8 * 8 + z % 8) * 2 + core) * 4 + x % 4


def far_groups():
    return [
        [spot(2 * y + a, 2 * z + b, core, 2 * x + d) for y in range(4) for z in range(4) for x in range(2)]
        for a in range(2)
        for b in range(2)
        for core in range(2)
        for d in range(2)
    ]


def near_groups():
    groups = []
    for core in range(2):
        pair = [[(k, 2 - k if odd else k) for k in range(2)] for odd in (core, core, 1 - core)]
        for y in range(4):
            for z in range(4):
                for x in range(2):
                    groups.append(
                        [
                            spot(2 * y + a[1], 2 * z + b[1], core, 2 * x + d[1])
                            for a in pair[0]
                            for b in pair[1]
                            for d in pair[2]
                        ]
                    )
    return groups


def exchange(blocks, groups):
    return lax.all_to_all(blocks, AXES, 0, 0, axis_index_groups=groups)


def swap_cores(block):
    count = lax.axis_size("seq")
    return lax.ppermute(block, "seq", [(i, i ^ 1) for i in range(count)])


def gather_far(w_block):
    far = exchange(jnp.broadcast_to(w_block, (32,) + w_block.shape), far_groups())
    return far.reshape(32 * w_block.shape[0], w_block.shape[1])


def gather_near(far):
    own = exchange(jnp.broadcast_to(far, (8,) + far.shape), near_groups())
    return own.reshape(8 * far.shape[0], far.shape[1])


def by_holder(x_local):
    tokens, width = x_local.shape
    rows = width // 512
    split = x_local.T.reshape(4, 2, 4, 2, 2, 2, 2, rows, tokens)
    return split.transpose(4, 1, 3, 6, 0, 2, 5, 7, 8).reshape(2, 256 * rows, tokens)


def in_order(own, other, core):
    rows, width = own.shape[0] // 256, own.shape[1]
    full = jnp.zeros((4, 2, 4, 2, 2, 2, 2, rows, width), own.dtype)
    for part, place in ((own, core), (other, 1 - core)):
        part = part.reshape(2, 2, 2, 4, 4, 2, rows, width).transpose(3, 0, 4, 1, 5, 2, 6, 7)
        full = lax.dynamic_update_slice_in_dim(full, part[:, :, :, :, None], place, 4)
    return full.reshape(512 * rows, width)


def scatter_near(total):
    rows, width = total.shape[0] // 8, total.shape[1]
    return exchange(total.reshape(8, rows, width), near_groups())


def scatter_far(blocks):
    total = jnp.sum(blocks.astype(jnp.float32), axis=0).astype(jnp.bfloat16)
    total = total.reshape(32, total.shape[0] // 32, total.shape[1])
    return jnp.sum(exchange(total, far_groups()).astype(jnp.float32), axis=0)


def dot32(a, b):
    return jnp.dot(a, b, preferred_element_type=jnp.float32)


def body(layer_inputs, doc_start, w_qkv, d_context):
    x_local = layer_inputs[0]
    tok_rows = x_local.shape[0]
    q_width = d_context.shape[2]
    head_dim = (w_qkv.shape[1] - q_width) // 2
    heads = q_width // head_dim
    out_grad = d_context[0].reshape(tok_rows, heads, head_dim)
    doc_first = doc_start[0]
    positions = lax.axis_index("seq") * tok_rows + jnp.arange(tok_rows, dtype=jnp.int32)
    core = lax.axis_index("seq") & 1
    x_rows = by_holder(x_local)
    rows_own = lax.dynamic_index_in_dim(x_rows, core, 0, keepdims=False)
    rows_other = lax.dynamic_index_in_dim(x_rows, 1 - core, 0, keepdims=False)
    far = gather_far(w_qkv)
    rows_own, rows_other, far = lax.optimization_barrier((rows_own, rows_other, far))
    x_own, x_other = rows_own.T, rows_other.T
    w_own = gather_near(far)
    w_other = swap_cores(w_own)
    projected = dot32(x_own, w_own) + dot32(x_other, w_other)
    projected = projected.astype(jnp.bfloat16)
    queries = projected[:, :q_width].reshape(tok_rows, heads, head_dim)
    key_value = projected[:, q_width:]
    prior = from_behind(key_value, "seq", 1)
    key_rows = jnp.concatenate([prior[:, :head_dim], key_value[:, :head_dim]], axis=0)
    value_rows = jnp.concatenate([prior[:, head_dim:], key_value[:, head_dim:]], axis=0)
    key_pos = jnp.concatenate([positions - tok_rows, positions])
    grad_query, grad_keys, grad_values, log_total, row_dot = local_pass(
        queries, key_rows, value_rows, out_grad, doc_first, positions, key_pos
    )
    returned = from_behind(
        jnp.concatenate([grad_keys[:tok_rows], grad_values[:tok_rows]], axis=1).astype(
            jnp.bfloat16
        ),
        "seq",
        -1,
    ).astype(jnp.float32)
    far_keys = returned[:, :head_dim]
    far_values = returned[:, head_dim:]
    key_grad = (grad_keys[tok_rows:] + far_keys).astype(jnp.bfloat16)
    value_grad = (grad_values[tok_rows:] + far_values).astype(jnp.bfloat16)
    low_query = grad_query.astype(jnp.bfloat16).reshape(tok_rows, q_width)
    low_kv = jnp.concatenate([key_grad, value_grad], axis=1)
    grad_proj = jnp.concatenate([low_query, low_kv], axis=1)
    received = [
        swap_cores(dot32(rows_other, part).astype(jnp.bfloat16)) for part in (low_query, low_kv)
    ]
    own = lax.optimization_barrier(dot32(rows_own, grad_proj).astype(jnp.bfloat16))
    total = own.astype(jnp.float32) + jnp.concatenate(received, axis=1).astype(jnp.float32)
    blocks = scatter_near(total.astype(jnp.bfloat16))
    blocks, w_own, w_other = lax.optimization_barrier((blocks, w_own, w_other))
    weight_grad = scatter_far(blocks)
    full_weights = in_order(w_own, w_other, core)
    input_grad = lax.dot_general(
        grad_proj, full_weights, (((1,), (1,)), ((), ())), preferred_element_type=jnp.float32
    )
    input_grad = input_grad.astype(jnp.bfloat16).reshape(1, tok_rows, x_local.shape[1])
    return (input_grad, weight_grad)


def solution(mesh):
    return jax.shard_map(
        body,
        mesh=mesh,
        in_specs=(
            P("dp", "seq", None),
            P("dp", "seq"),
            P(("seq", "dp"), None),
            P("dp", "seq", None),
        ),
        out_specs=(P("dp", "seq", None), P(("seq", "dp"), None)),
        check_vma=False,
    )
```

```python
import jax
import jax.numpy as jnp
from jax import lax
from jax.sharding import PartitionSpec as P

WIN = 256


def from_behind(block, axis, distance):
    devices = range(lax.axis_size(axis))
    route = [(i - distance, i) for i in devices if i - distance in devices]
    return lax.ppermute(block, axis, route)


def masked_scores(queries, key_rows, doc_first, query_pos, key_pos):
    inv_root = queries.shape[2] ** (-0.5)
    scores = (
        jnp.einsum("rhd,kd->hrk", queries, key_rows, preferred_element_type=jnp.float32) * inv_root
    )
    visible = (
        (key_pos[None, :] <= query_pos[:, None])
        & (key_pos[None, :] > query_pos[:, None] - WIN)
        & (key_pos[None, :] >= doc_first[:, None])
    )
    return jnp.where(visible[None, :, :], scores, -jnp.inf)


def backward_terms(queries, key_rows, value_rows, out_grad, attn_probs, prob_low, row_dot):
    inv_root = queries.shape[2] ** (-0.5)
    prob_grad = jnp.einsum("rhd,kd->hrk", out_grad, value_rows, preferred_element_type=jnp.float32)
    score_grad = (attn_probs * (prob_grad - row_dot[:, :, None])).astype(jnp.bfloat16)
    grad_query = (
        jnp.einsum("hrk,kd->rhd", score_grad, key_rows, preferred_element_type=jnp.float32)
        * inv_root
    )
    grad_keys = (
        jnp.einsum("hrk,rhd->kd", score_grad, queries, preferred_element_type=jnp.float32)
        * inv_root
    )
    grad_values = jnp.einsum("hrk,rhd->kd", prob_low, out_grad, preferred_element_type=jnp.float32)
    return (grad_query, grad_keys, grad_values)


def local_pass(queries, key_rows, value_rows, out_grad, doc_first, query_pos, key_pos):
    scores = masked_scores(queries, key_rows, doc_first, query_pos, key_pos)
    row_max = jnp.max(scores, axis=2)
    log_total = row_max + jnp.log(jnp.sum(jnp.exp(scores - row_max[:, :, None]), axis=2))
    attn_probs = jnp.exp(scores - log_total[:, :, None])
    prob_low = attn_probs.astype(jnp.bfloat16)
    context = jnp.einsum("hrk,kd->rhd", prob_low, value_rows, preferred_element_type=jnp.float32)
    row_dot = jnp.sum(out_grad.astype(jnp.float32) * context, axis=2).T
    grad_query, grad_keys, grad_values = backward_terms(
        queries, key_rows, value_rows, out_grad, attn_probs, prob_low, row_dot
    )
    return (grad_query, grad_keys, grad_values, log_total, row_dot)


AXES = ("seq", "dp")


def spot(y, z, core, x):
    return ((y % 8 * 8 + z % 8) * 2 + core) * 4 + x % 4


def far_groups():
    return [
        [spot(2 * y + a, 2 * z + b, core, 2 * x + d) for y in range(4) for z in range(4) for x in range(2)]
        for a in range(2)
        for b in range(2)
        for core in range(2)
        for d in range(2)
    ]


def near_groups():
    groups = []
    for core in range(2):
        for y in range(4):
            for z in range(4):
                for x in range(2):
                    low = [(k, k) if core == 0 else (k, 2 - k) for k in range(2)]
                    groups.append(
                        [
                            spot(2 * y + a[1], 2 * z + b[1], core, 2 * x + d[1])
                            for a in low
                            for b in low
                            for d in low
                        ]
                    )
    return groups


def exchange(blocks, groups):
    return lax.all_to_all(blocks, AXES, 0, 0, axis_index_groups=groups)


def swap_cores(block):
    count = lax.axis_size("seq")
    return lax.ppermute(block, "seq", [(i, i ^ 1) for i in range(count)])


def gather_far(w_block):
    far = exchange(jnp.broadcast_to(w_block, (32,) + w_block.shape), far_groups())
    return far.reshape(32 * w_block.shape[0], w_block.shape[1])


def gather_near(far):
    own = exchange(jnp.broadcast_to(far, (8,) + far.shape), near_groups())
    return own.reshape(8 * far.shape[0], far.shape[1])


def by_holder(x_local):
    tokens, width = x_local.shape
    rows = width // 512
    split = x_local.T.reshape(4, 2, 4, 2, 2, 2, 2, rows, tokens)
    return split.transpose(4, 1, 3, 6, 0, 2, 5, 7, 8).reshape(2, 256 * rows, tokens)


def in_order(own, other, core):
    rows, width = own.shape[0] // 256, own.shape[1]
    full = jnp.zeros((4, 2, 4, 2, 2, 2, 2, rows, width), own.dtype)
    for part, place in ((own, core), (other, 1 - core)):
        part = part.reshape(2, 2, 2, 4, 4, 2, rows, width).transpose(3, 0, 4, 1, 5, 2, 6, 7)
        full = lax.dynamic_update_slice_in_dim(full, part[:, :, :, :, None], place, 4)
    return full.reshape(512 * rows, width)


def scatter_near(total):
    rows, width = total.shape[0] // 8, total.shape[1]
    return exchange(total.reshape(8, rows, width), near_groups())


def scatter_far(blocks):
    total = jnp.sum(blocks.astype(jnp.float32), axis=0).astype(jnp.bfloat16)
    total = total.reshape(32, total.shape[0] // 32, total.shape[1])
    return jnp.sum(exchange(total, far_groups()).astype(jnp.float32), axis=0)


def dot32(a, b):
    return jnp.dot(a, b, preferred_element_type=jnp.float32)


def body(layer_inputs, doc_start, w_qkv, d_context):
    x_local = layer_inputs[0]
    tok_rows = x_local.shape[0]
    q_width = d_context.shape[2]
    head_dim = (w_qkv.shape[1] - q_width) // 2
    heads = q_width // head_dim
    out_grad = d_context[0].reshape(tok_rows, heads, head_dim)
    doc_first = doc_start[0]
    positions = lax.axis_index("seq") * tok_rows + jnp.arange(tok_rows, dtype=jnp.int32)
    core = lax.axis_index("seq") & 1
    x_rows = by_holder(x_local)
    rows_own = lax.dynamic_index_in_dim(x_rows, core, 0, keepdims=False)
    rows_other = lax.dynamic_index_in_dim(x_rows, 1 - core, 0, keepdims=False)
    far = gather_far(w_qkv)
    rows_own, rows_other, far = lax.optimization_barrier((rows_own, rows_other, far))
    x_own, x_other = rows_own.T, rows_other.T
    w_own = gather_near(far)
    w_other = swap_cores(w_own)
    partial = dot32(x_own, w_own)
    key_value = partial[:, q_width:] + dot32(x_other, w_other[:, q_width:])
    key_value = key_value.astype(jnp.bfloat16)
    prior = from_behind(key_value, "seq", 1)
    queries = partial[:, :q_width] + dot32(x_other, w_other[:, :q_width])
    queries = queries.astype(jnp.bfloat16).reshape(tok_rows, heads, head_dim)
    key_rows = jnp.concatenate([prior[:, :head_dim], key_value[:, :head_dim]], axis=0)
    value_rows = jnp.concatenate([prior[:, head_dim:], key_value[:, head_dim:]], axis=0)
    key_pos = jnp.concatenate([positions - tok_rows, positions])
    grad_query, grad_keys, grad_values, log_total, row_dot = local_pass(
        queries, key_rows, value_rows, out_grad, doc_first, positions, key_pos
    )
    returned = from_behind(
        jnp.concatenate([grad_keys[:tok_rows], grad_values[:tok_rows]], axis=1).astype(
            jnp.bfloat16
        ),
        "seq",
        -1,
    ).astype(jnp.float32)
    far_keys = returned[:, :head_dim]
    far_values = returned[:, head_dim:]
    key_grad = (grad_keys[tok_rows:] + far_keys).astype(jnp.bfloat16)
    value_grad = (grad_values[tok_rows:] + far_values).astype(jnp.bfloat16)
    low_query = grad_query.astype(jnp.bfloat16).reshape(tok_rows, q_width)
    low_kv = jnp.concatenate([key_grad, value_grad], axis=1)
    grad_proj = jnp.concatenate([low_query, low_kv], axis=1)
    received = [
        swap_cores(dot32(rows_other, part).astype(jnp.bfloat16)) for part in (low_query, low_kv)
    ]
    own = lax.optimization_barrier(dot32(rows_own, grad_proj).astype(jnp.bfloat16))
    total = own.astype(jnp.float32) + jnp.concatenate(received, axis=1).astype(jnp.float32)
    blocks = scatter_near(total.astype(jnp.bfloat16))
    blocks, w_own, w_other = lax.optimization_barrier((blocks, w_own, w_other))
    weight_grad = scatter_far(blocks)
    full_weights = in_order(w_own, w_other, core)
    input_grad = lax.dot_general(
        grad_proj, full_weights, (((1,), (1,)), ((), ())), preferred_element_type=jnp.float32
    )
    input_grad = input_grad.astype(jnp.bfloat16).reshape(1, tok_rows, x_local.shape[1])
    return (input_grad, weight_grad)


def solution(mesh):
    return jax.shard_map(
        body,
        mesh=mesh,
        in_specs=(
            P("dp", "seq", None),
            P("dp", "seq"),
            P(("seq", "dp"), None),
            P("dp", "seq", None),
        ),
        out_specs=(P("dp", "seq", None), P(("seq", "dp"), None)),
        check_vma=False,
    )
```
